128 devices in a mesh: ctx: 32 (over x, y, core), ch: 4 (over z).
Axes of the slice: x: 4, y: 4, z: 4, core: 2. Of those that a mesh axis runs over, the one named last changes fastest.
Arguments:
- grad_out: bfloat16 [16384, 8192], P(('ctx', 'ch')), may hold values from -6 to 6
- query_medium: bfloat16 [16384, 8192], P('ctx', 'ch'), may hold values from -6 to 6
- key_medium: bfloat16 [16384, 8192], P('ctx', 'ch'), may hold values from -6 to 6
- value_medium: bfloat16 [16384, 8192], P('ctx', 'ch'), may hold values from -6 to 6
- query_modal: bfloat16 [16384, 8192], P('ctx', 'ch'), may hold values from -6 to 6
- key_modal: bfloat16 [16384, 8192], P('ctx', 'ch'), may hold values from -6 to 6
- medium_filter: bfloat16 [512, 128], P('ch'), may hold values from -0.5 to 0.5
- modal_decay: float32 [512, 16], P('ch'), may hold values from 0 to 1
- modal_residue: float32 [512, 16], P('ch'), may hold values from -1 to 1
Outputs:
- grad_query_medium: bfloat16 [16384, 8192], P(('ctx', 'ch'))
- grad_key_medium: bfloat16 [16384, 8192], P(('ctx', 'ch'))
- grad_value_medium: bfloat16 [16384, 8192], P(('ctx', 'ch'))
- grad_query_modal: bfloat16 [16384, 8192], P(('ctx', 'ch'))
- grad_key_modal: bfloat16 [16384, 8192], P(('ctx', 'ch'))
- grad_medium_filter: float32 [512, 128], P('ch')
The draws below stay inside these ranges and needn't reach their ends.
All inputs are finite; a program needn't handle non-finite values.
Results may differ from the reference program's by a relative error of at most 0.015.
Values may be sent and summed in bfloat16 or wider, within the bound.
A program may use at most 192 MiB of HBM per device.

```python
import math
import jax
import jax.numpy as jnp
from jax import lax

D = 8192
GS = 16
TAPS = 128
MODES = 16
NEAR = 128
G = 512
SEQ = 16384


def modal_pair(key):
    base_key = jax.random.fold_in(key, 11)
    chooser_key, slow_key, middle_key, fast_key, residue_key = jax.random.split(base_key, 5)
    slow_share = 0.35
    middle_share = 0.35
    chooser = jax.random.uniform(chooser_key, (G, MODES), jnp.float32)
    slow_rate = jnp.exp(jax.random.uniform(slow_key, (G, MODES), jnp.float32, math.log(0.05 / SEQ), math.log(2.0 / SEQ)))
    middle_rate = jnp.exp(jax.random.uniform(middle_key, (G, MODES), jnp.float32, math.log(2.0 / SEQ), math.log(1.0 / 70.0)))
    fast_rate = jnp.exp(jax.random.uniform(fast_key, (G, MODES), jnp.float32, math.log(1.0 / 60.0), math.log(1.0 / 20.0)))
    decay_rate = jnp.where(chooser < slow_share, slow_rate, jnp.where(chooser < slow_share + middle_share, middle_rate, fast_rate))
    decay_value = jnp.exp(-decay_rate)
    residue = 0.25 * jax.random.normal(residue_key, (G, MODES), jnp.float32) * jnp.sqrt(1.0 - decay_value * decay_value + 1.0 / SEQ)
    return (decay_value, residue)


def draw_modal_decay(key, part):
    return modal_pair(key)[0]


def draw_modal_residue(key, part):
    return modal_pair(key)[1]


def level_of(key, extent, shards, low, top_value):
    factor_of, own = 1.0, jax.random.fold_in(key, 6)
    for dim, parts in shards:
        steps = jnp.exp(jax.random.uniform(jax.random.fold_in(own, dim), (parts,), jnp.float32, low / len(shards), top_value / len(shards)))
        factor_of = factor_of * jnp.repeat(steps, extent[dim] // parts).reshape([-1 if axis == dim else 1 for axis in range(len(extent))])
    return factor_of


def gaussian(stream_key, extent, width, limit, pieces=(), held_as=jnp.bfloat16):
    result = jax.random.normal(stream_key, extent, jnp.float32) * width
    if len(pieces) > 0:
        result = level_of(stream_key, extent, pieces, -0.22, 0.18) * result
    return jnp.clip(result, min=-limit, max=limit).astype(held_as)


def setup_inputs(seed: int = 0) -> dict:
    seeds = jax.random.split(jax.random.key(seed), 10)
    grad_out = gaussian(seeds[0], (SEQ, D), 1.0, 6.0, ((0, 128),))
    query_medium = gaussian(seeds[1], (SEQ, D), 1.0, 6.0, ((0, 32), (1, 4)))
    key_medium = gaussian(seeds[2], (SEQ, D), 1.0, 6.0, ((0, 32), (1, 4)))
    value_medium = gaussian(seeds[3], (SEQ, D), 1.0, 6.0, ((0, 32), (1, 4)))
    query_modal = gaussian(seeds[4], (SEQ, D), 1.0, 6.0, ((0, 32), (1, 4)))
    key_modal = gaussian(seeds[5], (SEQ, D), 1.0, 6.0, ((0, 32), (1, 4)))
    medium_filter = gaussian(seeds[6], (G, TAPS), TAPS ** -0.5, 0.5, ((0, 4),))
    modal_decay = draw_modal_decay(jax.random.fold_in(seeds[9], 71), 0)
    modal_residue = draw_modal_residue(jax.random.fold_in(seeds[9], 71), 0)
    return {"grad_out": grad_out, "query_medium": query_medium, "key_medium": key_medium, "value_medium": value_medium, "query_modal": query_modal, "key_modal": key_modal, "medium_filter": medium_filter, "modal_decay": modal_decay, "modal_residue": modal_residue}


highest = lax.Precision.HIGHEST

def skew_rows(vector, height):
    length = vector.shape[-1]
    leading = vector.shape[:-1]
    tiled_rows = jnp.broadcast_to(vector[..., None, :], leading + (height, length))
    tiled_rows = tiled_rows.reshape(leading + (height * length,))
    return tiled_rows[..., :height * (length - 1)].reshape(leading + (height, length - 1))

def medium_tables(medium_filter):
    groups = medium_filter.shape[0]
    tap_count = medium_filter.shape[1]
    front_zeros = jnp.zeros((groups, tap_count + 1), medium_filter.dtype)
    back_zeros = jnp.zeros((groups, tap_count), medium_filter.dtype)
    vector = jnp.concatenate([front_zeros, medium_filter[:, ::-1], back_zeros], axis=1)
    toeplitz = skew_rows(vector, tap_count)[:, :, tap_count:]
    return (toeplitz[:, :, :tap_count], toeplitz[:, :, tap_count:])

def near_table(near_taps):
    groups = near_taps.shape[0]
    count = near_taps.shape[1]
    front_zeros = jnp.zeros((groups, 1), near_taps.dtype)
    back_zeros = jnp.zeros((groups, count), near_taps.dtype)
    vector = jnp.concatenate([front_zeros, near_taps[:, ::-1], back_zeros], axis=1)
    return skew_rows(vector, count)[:, :, count:]

def diagonal_sums(products):
    groups, height, length = products.shape
    flat_values = products.reshape(groups, height * length)
    flat_values = jnp.concatenate([flat_values, jnp.zeros((groups, height), products.dtype)], axis=1)
    shifted = flat_values.reshape(groups, height, length + 1)
    return lax.optimization_barrier(jnp.sum(shifted[:, :, 1:height + 1], axis=1))[:, ::-1]

def modal_tables(modal_decay, modal_residue):
    log_decay = jnp.log(modal_decay)
    lags = jnp.arange(NEAR).astype(jnp.float32)
    powers = jnp.exp(log_decay[:, :, None] * lags)
    taps_full = lax.optimization_barrier(jnp.sum(modal_residue[:, :, None] * powers, axis=1))
    near_taps = taps_full.astype(jnp.bfloat16)
    end_weight = jnp.exp(log_decay[:, :, None] * (NEAR - 1 - lags))
    out_weight = modal_residue[:, :, None] * jnp.exp(log_decay[:, :, None] * (lags + 1.0))
    back_weight = modal_residue[:, :, None] * jnp.exp(log_decay[:, :, None] * (NEAR - lags))
    step_decay = jnp.exp(log_decay * NEAR)[:, None, :]
    return (near_taps, end_weight, powers, out_weight, back_weight, step_decay)

def blocked(values, height):
    return values.reshape(values.shape[0] // height, height, values.shape[1] // GS, GS)

def flat_rows(values):
    return values.reshape(values.shape[0] * values.shape[1], values.shape[2] * values.shape[3])

def medium_apply(prev_tab, curr_tab, earlier_rows, current_rows):
    front_part = jnp.einsum('grs,bsgc->brgc', prev_tab.astype(jnp.float32), blocked(earlier_rows, TAPS).astype(jnp.float32))
    back_part = jnp.einsum('grs,bsgc->brgc', curr_tab.astype(jnp.float32), blocked(current_rows, TAPS).astype(jnp.float32))
    return flat_rows(front_part + back_part)

def medium_adjoint(prev_tab, curr_tab, current_grad, later_grad):
    own_part = jnp.einsum('grs,brgc->bsgc', curr_tab.astype(jnp.float32), blocked(current_grad, TAPS).astype(jnp.float32))
    next_part = jnp.einsum('grs,brgc->bsgc', prev_tab.astype(jnp.float32), blocked(later_grad, TAPS).astype(jnp.float32))
    return flat_rows(own_part + next_part)

def medium_products(grad_conv, earlier_rows, current_rows):
    grad_blocks = blocked(grad_conv, TAPS).astype(jnp.float32)
    front_part = jnp.einsum('brgc,bsgc->grs', grad_blocks, blocked(earlier_rows, TAPS).astype(jnp.float32))
    back_part = jnp.einsum('brgc,bsgc->grs', grad_blocks, blocked(current_rows, TAPS).astype(jnp.float32))
    return jnp.concatenate([front_part, back_part], axis=2)

def reference(grad_out, query_medium, key_medium, value_medium, query_modal, key_modal, medium_filter, modal_decay, modal_residue):
    row_count = query_medium.shape[0]
    channels = query_medium.shape[1]
    prev_tab, curr_tab = medium_tables(medium_filter)
    medium_input = (key_medium.astype(jnp.float32) * value_medium.astype(jnp.float32)).astype(jnp.bfloat16)
    earlier_rows = jnp.concatenate([jnp.zeros((TAPS, channels), jnp.bfloat16), medium_input[:row_count - TAPS]], axis=0)
    medium_conv = medium_apply(prev_tab, curr_tab, earlier_rows, medium_input)
    medium_out = (query_medium.astype(jnp.float32) * medium_conv).astype(jnp.bfloat16)
    modal_input = (key_modal.astype(jnp.float32) * medium_out.astype(jnp.float32)).astype(jnp.bfloat16)
    near_taps, end_weight, start_weight, out_weight, back_weight, step_decay = modal_tables(modal_decay, modal_residue)
    near_tab = near_table(near_taps).astype(jnp.float32)
    input_blocks = blocked(modal_input, NEAR).astype(jnp.float32)
    end_states = jnp.einsum('gns,bsgc->bgcn', end_weight, input_blocks, precision=highest)
    zero_state = jnp.zeros(end_states.shape[1:], jnp.float32)

    def forward_step(carried, end_state):
        return (step_decay * carried + end_state, carried)
    unused, befores = lax.scan(forward_step, zero_state, end_states)
    far_part = jnp.einsum('gnr,bgcn->brgc', out_weight, befores, precision=highest)
    near_part = jnp.einsum('grs,bsgc->brgc', near_tab, input_blocks)
    modal_conv = flat_rows(near_part + far_part)
    cotangent = grad_out.astype(jnp.float32)
    grad_query_modal = (cotangent * modal_conv).astype(jnp.bfloat16)
    grad_modal_conv = (cotangent * query_modal.astype(jnp.float32)).astype(jnp.bfloat16)
    grad_blocks = blocked(grad_modal_conv, NEAR).astype(jnp.float32)
    start_states = jnp.einsum('gnr,brgc->bgcn', start_weight, grad_blocks, precision=highest)

    def backward_step(carried, start_state):
        return (step_decay * carried + start_state, carried)
    unused_back, nexts = lax.scan(backward_step, zero_state, start_states, reverse=True)
    near_back = jnp.einsum('grs,brgc->bsgc', near_tab, grad_blocks)
    far_back = jnp.einsum('gns,bgcn->bsgc', back_weight, nexts, precision=highest)
    grad_modal_input = flat_rows(near_back + far_back)
    grad_key_modal = (grad_modal_input * medium_out.astype(jnp.float32)).astype(jnp.bfloat16)
    grad_medium_out = grad_modal_input * key_modal.astype(jnp.float32)
    grad_query_medium = (grad_medium_out * medium_conv).astype(jnp.bfloat16)
    grad_medium_conv = (grad_medium_out * query_medium.astype(jnp.float32)).astype(jnp.bfloat16)
    later_rows = jnp.concatenate([grad_medium_conv[TAPS:], jnp.zeros((TAPS, channels), jnp.bfloat16)], axis=0)
    grad_medium_input = medium_adjoint(prev_tab, curr_tab, grad_medium_conv, later_rows)
    grad_key_medium = (grad_medium_input * value_medium.astype(jnp.float32)).astype(jnp.bfloat16)
    grad_value_medium = (grad_medium_input * key_medium.astype(jnp.float32)).astype(jnp.bfloat16)
    products = medium_products(grad_medium_conv, earlier_rows, medium_input)
    grad_medium_filter = diagonal_sums(products) * (1.0 / math.sqrt(row_count * GS))
    return (grad_query_medium, grad_key_medium, grad_value_medium, grad_query_modal, grad_key_modal, grad_medium_filter)
```

```python
import math

import jax
import jax.numpy as jnp
from jax import lax
from jax.experimental import pallas as pl
from jax.experimental.pallas import tpu as pltpu
from jax.sharding import PartitionSpec as P

GS = 16
TAPS = 128
NEAR = 128
LANES = 128
TILE_GROUPS = LANES // GS
MESH = pl.DeviceIdType.MESH

f32 = jnp.float32
bf16 = jnp.bfloat16


def dot(a, b):
    return jnp.dot(a, b, preferred_element_type=f32)


def lane_group(rows, columns):
    lane = lax.broadcasted_iota(jnp.int32, (rows, columns), 1)
    return jnp.bitwise_and(lax.shift_right_logical(lane, 4), TILE_GROUPS - 1)


def pick(stacked, rows, columns):
    group = lane_group(rows, columns)
    kept = stacked[0:rows]
    for g in range(1, TILE_GROUPS):
        kept = jnp.where(group == g, stacked[g * rows : (g + 1) * rows], kept)
    return kept


def skewed(row, height):
    wide = jnp.broadcast_to(row, (height, row.shape[1]))
    return pltpu.roll(wide, 0, 1, stride=1, stride_axis=0)


def split(value):
    high = value.astype(bf16)
    return high, (value - high.astype(f32)).astype(bf16)


def block_states(weight, data):
    high, low = split(weight)
    left = jnp.concatenate([high, low], axis=1)
    right = jnp.concatenate([data, data], axis=0)
    modes = weight.shape[0] // TILE_GROUPS
    return pick(dot(left, right), modes, data.shape[1])


def side_by_side(values, blocks):
    return jnp.concatenate([values[NEAR * b : NEAR * (b + 1)] for b in range(blocks)], axis=1)


def conv_pair(table_ref, data_ref, pair):
    low = 2 * pair * NEAR
    right = jnp.concatenate(
        [data_ref[low : low + 2 * NEAR], data_ref[low + NEAR : low + 3 * NEAR]], axis=1
    )
    return pick(dot(table_ref[...], right), NEAR, 2 * LANES)


def forward_kernel(
    key_ref, value_ref, query_ref, key_modal_ref, halo_ref, row_ref, log_ref, step_ref,
    conv_ref, out_ref, states_ref, total_ref, table_ref, data_ref,
):
    blocks = key_ref.shape[0] // NEAR
    for g in range(TILE_GROUPS):
        table_ref[NEAR * g : NEAR * (g + 1)] = skewed(row_ref[g : g + 1], NEAR).astype(bf16)
    data_ref[0:NEAR] = halo_ref[...]
    data_ref[NEAR:] = (key_ref[...].astype(f32) * value_ref[...].astype(f32)).astype(bf16)
    inputs = []
    for pair in range(blocks // 2):
        both = conv_pair(table_ref, data_ref, pair)
        for half in range(2):
            rows = slice(NEAR * (2 * pair + half), NEAR * (2 * pair + half + 1))
            conv = both[:, LANES * half : LANES * (half + 1)]
            conv_ref[rows] = conv
            out = (query_ref[rows].astype(f32) * conv).astype(bf16)
            out_ref[rows] = out
            inputs.append((key_modal_ref[rows].astype(f32) * out.astype(f32)).astype(bf16))
    lag = lax.broadcasted_iota(jnp.int32, (NEAR, NEAR), 1).astype(f32)
    weight = jnp.exp(log_ref[...] * (NEAR - 1 - lag))
    states = block_states(weight, jnp.concatenate(inputs, axis=1))
    total = jnp.zeros_like(total_ref)
    for b in range(blocks):
        state = states[:, LANES * b : LANES * (b + 1)]
        states_ref[b] = state
        total = step_ref[...] * total + state
    total_ref[...] = total


def adjoint_state_kernel(cotangent_ref, query_modal_ref, log_ref, step_ref, states_ref, total_ref):
    blocks = cotangent_ref.shape[0] // NEAR
    grad = (cotangent_ref[...].astype(f32) * query_modal_ref[...].astype(f32)).astype(bf16)
    lag = lax.broadcasted_iota(jnp.int32, (NEAR, NEAR), 1).astype(f32)
    states = block_states(jnp.exp(log_ref[...] * lag), side_by_side(grad, blocks))
    total = jnp.zeros_like(total_ref)
    for b in reversed(range(blocks)):
        state = states[:, LANES * b : LANES * (b + 1)]
        states_ref[b] = state
        total = step_ref[...] * total + state
    total_ref[...] = total


def fill_modal_table(table_ref, taps_ref, log_ref, residue_ref, adjoint):
    row = lax.broadcasted_iota(jnp.int32, (NEAR, LANES), 0)
    lane = lax.broadcasted_iota(jnp.int32, (NEAR, LANES), 1)
    near = row <= lane if adjoint else lane <= row
    lag = ((NEAR - row) if adjoint else (row + 1)).astype(f32)
    for g in range(TILE_GROUPS):
        taps = jnp.where(near, skewed(taps_ref[g : g + 1], NEAR), 0.0)
        far = residue_ref[g : g + 1] * jnp.exp(log_ref[g : g + 1] * lag)
        high = far.astype(bf16).astype(f32)
        far = jnp.where(lane < 32, high, far - high)
        rows = slice(NEAR * g, NEAR * (g + 1))
        table_ref[rows, 0:LANES] = taps.astype(bf16)
        table_ref[rows, LANES:] = far.astype(bf16)


def modal_blocks(table_ref, data_ref, states):
    high, low = split(states)
    modes = states.shape[0]
    data_ref[NEAR : NEAR + modes] = high
    data_ref[NEAR + modes : NEAR + 2 * modes] = low
    data_ref[NEAR + 2 * modes : NEAR + 3 * modes] = high
    data_ref[NEAR + 3 * modes :] = jnp.zeros(
        (NEAR - 3 * modes, data_ref.shape[1]), data_ref.dtype
    )
    parts = []
    for pair in range(data_ref.shape[1] // (2 * LANES)):
        right = data_ref[:, 2 * LANES * pair : 2 * LANES * (pair + 1)]
        both = pick(dot(table_ref[...], right), NEAR, 2 * LANES)
        parts += [both[:, 0:LANES], both[:, LANES:]]
    return parts


def modal_kernel(
    cotangent_ref, key_modal_ref, out_ref, states_ref, entering_ref, step_ref,
    taps_ref, log_ref, residue_ref, grad_ref, table_ref, data_ref,
):
    blocks = cotangent_ref.shape[0] // NEAR
    fill_modal_table(table_ref, taps_ref, log_ref, residue_ref, False)
    carried = entering_ref[...]
    befores = []
    for b in range(blocks):
        rows = slice(NEAR * b, NEAR * (b + 1))
        data_ref[0:NEAR, LANES * b : LANES * (b + 1)] = (
            key_modal_ref[rows].astype(f32) * out_ref[rows].astype(f32)
        ).astype(bf16)
        befores.append(carried)
        carried = step_ref[...] * carried + states_ref[b]
    parts = modal_blocks(table_ref, data_ref, jnp.concatenate(befores, axis=1))
    for b in range(blocks):
        rows = slice(NEAR * b, NEAR * (b + 1))
        grad_ref[rows] = (cotangent_ref[rows].astype(f32) * parts[b]).astype(bf16)


def modal_adjoint_kernel(
    cotangent_ref, query_modal_ref, key_modal_ref, query_ref, conv_ref, out_ref,
    states_ref, entering_ref, step_ref, taps_ref, log_ref, residue_ref,
    grad_key_modal_ref, grad_query_ref, grad_conv_ref, table_ref, data_ref,
):
    blocks = cotangent_ref.shape[0] // NEAR
    fill_modal_table(table_ref, taps_ref, log_ref, residue_ref, True)
    carried = entering_ref[...]
    nexts = [carried] * blocks
    for b in reversed(range(blocks)):
        rows = slice(NEAR * b, NEAR * (b + 1))
        data_ref[0:NEAR, LANES * b : LANES * (b + 1)] = (
            cotangent_ref[rows].astype(f32) * query_modal_ref[rows].astype(f32)
        ).astype(bf16)
        nexts[b] = carried
        carried = step_ref[...] * carried + states_ref[b]
    parts = modal_blocks(table_ref, data_ref, jnp.concatenate(nexts, axis=1))
    for b in range(blocks):
        rows = slice(NEAR * b, NEAR * (b + 1))
        grad_key_modal_ref[rows] = (parts[b] * out_ref[rows].astype(f32)).astype(bf16)
        grad_out = parts[b] * key_modal_ref[rows].astype(f32)
        grad_query_ref[rows] = (grad_out * conv_ref[rows]).astype(bf16)
        grad_conv_ref[rows] = (grad_out * query_ref[rows].astype(f32)).astype(bf16)


def medium_adjoint_kernel(
    grad_ref, halo_ref, key_ref, value_ref, row_ref,
    grad_key_ref, grad_value_ref, table_ref, data_ref,
):
    blocks = grad_ref.shape[0] // NEAR
    for g in range(TILE_GROUPS):
        table_ref[NEAR * g : NEAR * (g + 1)] = skewed(row_ref[g : g + 1], NEAR).astype(bf16)
    data_ref[0 : NEAR * blocks] = grad_ref[...]
    data_ref[NEAR * blocks :] = halo_ref[...]
    for pair in range(blocks // 2):
        both = conv_pair(table_ref, data_ref, pair)
        for half in range(2):
            rows = slice(NEAR * (2 * pair + half), NEAR * (2 * pair + half + 1))
            grad_input = both[:, LANES * half : LANES * (half + 1)]
            grad_key_ref[rows] = (grad_input * value_ref[rows].astype(f32)).astype(bf16)
            grad_value_ref[rows] = (grad_input * key_ref[rows].astype(f32)).astype(bf16)


def product_kernel(grad_ref, key_ref, value_ref, halo_ref, sums_ref, left_ref, data_ref):
    blocks = grad_ref.shape[0] // NEAR
    data_ref[0:NEAR] = halo_ref[...]
    data_ref[NEAR:] = (key_ref[...].astype(f32) * value_ref[...].astype(f32)).astype(bf16)
    row = lax.broadcasted_iota(jnp.int32, (NEAR, NEAR), 0)
    lane = lax.broadcasted_iota(jnp.int32, (NEAR, NEAR), 1)
    flip = jnp.where(row + lane == NEAR - 1, 1.0, 0.0).astype(bf16)
    flipped = dot(flip, side_by_side(grad_ref[...], blocks))
    group = lane_group(NEAR, blocks * LANES)
    for g in range(TILE_GROUPS):
        left_ref[NEAR * g : NEAR * (g + 1)] = jnp.where(group == g, flipped, 0.0).astype(bf16)
    right = jnp.concatenate(
        [data_ref[NEAR * b : NEAR * (b + 2)] for b in range(blocks)], axis=1
    )
    products = lax.dot_general(
        left_ref[...], right, (((1,), (1,)), ((), ())), preferred_element_type=f32
    )
    for g in range(TILE_GROUPS):
        turned = pltpu.roll(
            products[NEAR * g : NEAR * (g + 1)], 0, 1, stride=1, stride_axis=0
        )
        sums_ref[g : g + 1] = jnp.sum(turned[:, NEAR:], axis=0, keepdims=True)


def join_kernel(grid, total_ref, adjoint_ref, log_ref, entering_ref, arriving_ref,
                slots, pair_ref, send_sem, recv_sem):
    size_x, size_y, _ = grid
    me = lax.axis_index("ctx")
    core = lax.rem(me, 2)
    y = lax.rem(lax.div(me, 2), size_y)
    x = lax.div(me, 2 * size_y)

    def index(a, b, c):
        return (a * size_y + b) * 2 + c

    partner = index(x, y, 1 - core)
    y_peers = [index(x, lax.rem(y + k, size_y), core) for k in range(1, size_y)]
    x_peers = [index(lax.rem(x + k, size_x), y, core) for k in range(1, size_x)]
    peers = [partner] + y_peers + x_peers
    barrier = pltpu.get_barrier_semaphore()
    for peer in peers:
        pl.semaphore_signal(barrier, inc=1, device_id={"ctx": peer}, device_id_type=MESH)
    pl.semaphore_wait(barrier, len(peers))

    def send(source, target, slot, peer):
        copy = pltpu.make_async_remote_copy(
            src_ref=source, dst_ref=target, send_sem=send_sem.at[slot],
            recv_sem=recv_sem.at[slot], device_id={"ctx": peer}, device_id_type=MESH,
        )
        copy.start()
        return copy

    log = log_ref[...]
    rows = log_ref.shape

    def decay(steps):
        return jnp.where(steps == 0, 1.0, jnp.exp(log * (steps * 1.0)))

    span = TAPS * 4
    first = send(total_ref, pair_ref.at[0], 0, partner)
    second = send(adjoint_ref, pair_ref.at[1], 1, partner)
    one = jnp.exp(log * span)
    first.wait()
    second.wait()
    forward = core == 0
    mine = jnp.where(forward, total_ref[...], adjoint_ref[...])
    theirs = jnp.where(forward, pair_ref[0], pair_ref[1])
    slots[0] = one * mine + theirs

    def stage(base, peers, place, count, chip_steps):
        copies = [
            send(slots.at[base], slots.at[base + k + 1], 2 + base + k, peer)
            for k, peer in enumerate(peers)
        ]
        for copy in copies:
            copy.wait()
        before = jnp.zeros(rows, f32)
        whole = jnp.zeros(rows, f32)
        for k in range(count):
            source = lax.rem(place - k + count, count)
            value = slots[base + k]
            gap = jnp.where(forward, place - source - 1, source - place - 1)
            rest = jnp.where(forward, count - 1 - source, source)
            near = gap >= 0
            weight = decay(jnp.where(near, gap, 0) * (chip_steps * 2 * span))
            before = before + jnp.where(near, weight * value, 0.0)
            whole = whole + decay(rest * (chip_steps * 2 * span)) * value
        return before, whole

    before_y, whole_y = stage(0, y_peers, y, size_y, 1)
    slots[size_y] = whole_y
    before_x, _ = stage(size_y, x_peers, x, size_x, size_y)
    inner = jnp.where(forward, y, size_y - 1 - y)
    before = before_y + decay(inner * (2 * span)) * before_x
    pair_ref[2] = before
    last = send(pair_ref.at[2], pair_ref.at[3], 2 + size_x + size_y, partner)
    last.wait()
    other = pair_ref[3]
    entering_ref[...] = jnp.where(forward, before, one * other + pair_ref[0])
    arriving_ref[...] = jnp.where(forward, one * other + pair_ref[1], before)


def tile_spec(rows):
    return pl.BlockSpec((rows, LANES), lambda i: (0, i))


def group_spec(columns):
    return pl.BlockSpec((TILE_GROUPS, columns), lambda i: (i, 0))


def call(body, tiles, in_specs, outs, out_specs, scratch, flops, *args):
    moved = sum(math.prod(a.shape) * a.dtype.itemsize for a in list(args) + list(outs))
    return pl.pallas_call(
        body,
        grid=(tiles,),
        in_specs=in_specs,
        out_shape=outs,
        out_specs=out_specs,
        scratch_shapes=scratch,
        cost_estimate=pl.CostEstimate(flops=flops, bytes_accessed=moved, transcendentals=0),
    )(*args)


def on_device(
    sizes,
    grad_out,
    query_medium,
    key_medium,
    value_medium,
    query_modal,
    key_modal,
    medium_filter,
    modal_decay,
    modal_residue,
):
    row_count, channels = query_medium.shape
    blocks = row_count // NEAR
    tiles = channels // LANES
    groups, modes = modal_decay.shape
    devices = lax.axis_size("ctx")
    data = jax.ShapeDtypeStruct((row_count, channels), bf16)
    data32 = jax.ShapeDtypeStruct((row_count, channels), f32)
    states_shape = jax.ShapeDtypeStruct((blocks, modes, channels), f32)
    state_shape = jax.ShapeDtypeStruct((modes, channels), f32)
    column = tile_spec(row_count)
    halo = tile_spec(NEAR)
    state = tile_spec(modes)
    states = pl.BlockSpec((blocks, modes, LANES), lambda i: (0, 0, i))
    log_block = pl.BlockSpec((TILE_GROUPS * modes, NEAR), lambda i: (i, 0))
    wide_table = pltpu.VMEM((TILE_GROUPS * NEAR, 2 * NEAR), bf16)
    long_data = pltpu.VMEM((row_count + NEAR, LANES), bf16)
    wide_data = pltpu.VMEM((2 * NEAR, blocks * LANES), bf16)
    work = 2 * tiles * TILE_GROUPS * NEAR * 2 * NEAR * blocks * LANES

    cotangent = lax.all_to_all(grad_out, "ch", split_axis=1, concat_axis=0, tiled=True)

    tail = (
        key_medium[row_count - TAPS :].astype(f32) * value_medium[row_count - TAPS :].astype(f32)
    ).astype(bf16)
    tail = lax.ppermute(tail, "ctx", [(i, i + 1) for i in range(devices - 1)])

    filter32 = medium_filter.astype(f32)
    no_taps = jnp.zeros_like(filter32)
    forward_row = jnp.concatenate(
        [no_taps[:, :1], filter32[:, ::-1], no_taps[:, : TAPS - 1]], axis=1
    )
    adjoint_row = jnp.concatenate([filter32, no_taps], axis=1)
    log_decay = jnp.log(modal_decay)
    lags = jnp.arange(NEAR).astype(f32)
    taps = jnp.sum(modal_residue[:, :, None] * jnp.exp(log_decay[:, :, None] * lags), axis=1)
    taps = taps.astype(bf16).astype(f32)
    taps_back = jnp.concatenate([taps[:, :1], taps[:, :0:-1]], axis=1)
    log_columns = jnp.broadcast_to(log_decay.reshape(groups * modes, 1), (groups * modes, NEAR))

    def three(value):
        return jnp.concatenate([value] * 3 + [jnp.zeros((groups, LANES - 3 * modes), f32)], axis=1)

    log_three, residue_three = three(log_decay), three(modal_residue)
    log_rows = jnp.repeat(log_decay.T, GS, axis=1)
    step = jnp.exp(log_rows * NEAR)

    conv, medium_out, end_states, own_total = call(
        forward_kernel, tiles,
        [column] * 4 + [halo, group_spec(2 * TAPS), log_block, state],
        (data32, data, states_shape, state_shape), (column, column, states, state),
        [wide_table, long_data], work,
        key_medium, value_medium, query_medium, key_modal, tail, forward_row, log_columns, step,
    )
    start_states, own_adjoint = call(
        adjoint_state_kernel, tiles, [column] * 2 + [log_block, state],
        (states_shape, state_shape), (states, state), [], work // 8,
        cotangent, query_modal, log_columns, step,
    )
    size_x, size_y, _ = sizes
    vmem = pl.BlockSpec(memory_space=pltpu.VMEM)
    entering, arriving = pl.pallas_call(
        lambda *refs: join_kernel(sizes, *refs),
        in_specs=[vmem] * 3,
        out_shape=(state_shape, state_shape),
        out_specs=(vmem, vmem),
        scratch_shapes=[
            pltpu.VMEM((size_x + size_y, modes, channels), f32),
            pltpu.VMEM((4, modes, channels), f32),
            pltpu.SemaphoreType.DMA((3 + size_x + size_y,)),
            pltpu.SemaphoreType.DMA((3 + size_x + size_y,)),
        ],
        compiler_params=pltpu.CompilerParams(collective_id=0, has_side_effects=True),
    )(own_total, own_adjoint, log_rows)

    modal_specs = [states, state, state, group_spec(NEAR), group_spec(LANES), group_spec(LANES)]
    (grad_query_modal,) = call(
        modal_kernel, tiles, [column] * 3 + modal_specs, (data,), (column,),
        [wide_table, wide_data], work,
        cotangent, key_modal, medium_out, end_states, entering, step,
        taps_back, log_three, residue_three,
    )

    def home(value):
        return lax.all_to_all(value, "ch", split_axis=0, concat_axis=1, tiled=True)

    grad_query_modal = home(grad_query_modal)
    grad_key_modal, grad_query, grad_conv = call(
        modal_adjoint_kernel, tiles, [column] * 6 + modal_specs, (data,) * 3, (column,) * 3,
        [wide_table, wide_data], work,
        cotangent, query_modal, key_modal, query_medium, conv, medium_out,
        start_states, arriving, step, taps, log_three, residue_three,
    )
    head = lax.ppermute(grad_conv[:TAPS], "ctx", [(i + 1, i) for i in range(devices - 1)])
    grad_key_modal = home(grad_key_modal)
    grad_query = home(grad_query)
    (sums,) = call(
        product_kernel, tiles, [column] * 3 + [halo],
        (jax.ShapeDtypeStruct((groups, NEAR), f32),), (group_spec(NEAR),),
        [pltpu.VMEM((TILE_GROUPS * NEAR, blocks * LANES), bf16), long_data], work,
        grad_conv, key_medium, value_medium, tail,
    )
    grad_key, grad_value = call(
        medium_adjoint_kernel, tiles,
        [column, halo, column, column, group_spec(2 * TAPS)],
        (data, data), (column, column), [wide_table, long_data], work,
        grad_conv, head, key_medium, value_medium, adjoint_row,
    )
    filter_scale = 1.0 / math.sqrt(row_count * devices * GS)
    grad_filter = lax.psum(sums[:, ::-1], "ctx") * filter_scale
    return (grad_query, home(grad_key), home(grad_value), grad_query_modal, grad_key_modal,
            grad_filter)


def solution(mesh):
    count = mesh.shape["ctx"] // 2
    side = math.isqrt(count)
    sizes = (side, count // side, 2)

    def body(*args):
        return on_device(sizes, *args)

    rows = P(("ctx", "ch"), None)
    groups = P("ch", None)
    return jax.shard_map(
        body,
        mesh=mesh,
        in_specs=(rows,) + (P("ctx", "ch"),) * 5 + (groups,) * 3,
        out_specs=(rows,) * 5 + (groups,),
        check_vma=False,
    )
```

```python
import math

import jax
import jax.numpy as jnp
from jax import lax
from jax.experimental import pallas as pl
from jax.experimental.pallas import tpu as pltpu
from jax.sharding import PartitionSpec as P

GS = 16
TAPS = 128
NEAR = 128
LANES = 128
TILE_GROUPS = LANES // GS
CHUNKS = 4
MESH = pl.DeviceIdType.MESH

f32 = jnp.float32
bf16 = jnp.bfloat16
highest = lax.Precision.HIGHEST


def dot(a, b):
    return jnp.dot(a, b, preferred_element_type=f32)


def iota(shape, axis):
    return lax.broadcasted_iota(jnp.int32, shape, axis)


def ramp(axis):
    return iota((NEAR, LANES), axis)


def lane_group(rows, columns):
    lane = iota((rows, columns), 1)
    return jnp.bitwise_and(lax.shift_right_logical(lane, 4), TILE_GROUPS - 1)


def pick(stacked, rows, columns):
    group = lane_group(rows, columns)
    kept = stacked[0:rows]
    for g in range(1, TILE_GROUPS):
        kept = jnp.where(group == g, stacked[g * rows : (g + 1) * rows], kept)
    return kept


def skewed(row, height):
    wide = jnp.broadcast_to(row, (height, row.shape[1]))
    return pltpu.roll(wide, 0, 1, stride=1, stride_axis=0)


def split(value):
    high = value.astype(bf16)
    return high, (value - high.astype(f32)).astype(bf16)


def product(a, b):
    return (a.astype(f32) * b.astype(f32)).astype(bf16)


def block_rows(b):
    return slice(NEAR * b, NEAR * (b + 1))


def block_states(weight, data):
    high, low = split(weight.T)
    left = jnp.concatenate([high, low], axis=1)
    right = jnp.concatenate([data, data], axis=0)
    return pick(dot(left, right), weight.shape[1] // TILE_GROUPS, data.shape[1])


def fill_medium_table(table_ref, row_ref, tile):
    rows = row_ref[pl.ds(pl.multiple_of(tile * TILE_GROUPS, TILE_GROUPS), TILE_GROUPS)]
    for g in range(TILE_GROUPS):
        table_ref[block_rows(g)] = skewed(rows[g : g + 1], NEAR).astype(bf16)


def medium_pair(table_ref, data_ref, lanes, pair):
    low = 2 * pair * NEAR
    right = jnp.concatenate(
        [data_ref[low : low + 2 * NEAR, lanes], data_ref[low + NEAR : low + 3 * NEAR, lanes]],
        axis=1,
    )
    return pick(dot(table_ref[...], right), NEAR, 2 * LANES)


def fill_modal_table(table_ref, log_row, residue_row, modes, adjoint):
    row, lane = ramp(0), ramp(1)
    lag = row if adjoint else jnp.bitwise_and(NEAR - row, NEAR - 1)
    terms = residue_row * jnp.exp(log_row * lag.astype(f32))
    member = jnp.where(lane_group(TILE_GROUPS, LANES) == iota((TILE_GROUPS, LANES), 0), 1.0, 0.0)
    taps = lax.dot_general(
        member, terms, (((1,), (1,)), ((), ())), precision=highest, preferred_element_type=f32
    )
    small = iota((TILE_GROUPS, LANES), 1)

    def three(value):
        turned = pltpu.roll(
            jnp.broadcast_to(value, (TILE_GROUPS, LANES)), 0, 1, stride=modes, stride_axis=0
        )
        again, third = pltpu.roll(turned, modes, 1), pltpu.roll(turned, 2 * modes, 1)
        return jnp.where(small < modes, turned, jnp.where(small < 2 * modes, again, third))

    logs, residues = three(log_row), jnp.where(small < 3 * modes, three(residue_row), 0.0)
    near = row <= lane if adjoint else lane <= row
    far_lag = ((NEAR - row) if adjoint else (row + 1)).astype(f32)
    for g in range(TILE_GROUPS):
        q = (TILE_GROUPS - g) % TILE_GROUPS
        table_ref[block_rows(g), 0:LANES] = jnp.where(
            near, skewed(taps[g : g + 1], NEAR), 0.0
        ).astype(bf16)
        far = residues[q : q + 1] * jnp.exp(logs[q : q + 1] * far_lag)
        high = far.astype(bf16).astype(f32)
        table_ref[block_rows(g), LANES:] = jnp.where(
            lane < 2 * modes, high, far - high
        ).astype(bf16)


def modal_blocks(table_ref, data_ref, states):
    high, low = split(states)
    modes = states.shape[0]
    data_ref[NEAR : NEAR + modes] = high
    data_ref[NEAR + modes : NEAR + 2 * modes] = low
    data_ref[NEAR + 2 * modes : NEAR + 3 * modes] = high
    parts = []
    for pair in range(data_ref.shape[1] // (2 * LANES)):
        right = data_ref[:, 2 * LANES * pair : 2 * LANES * (pair + 1)]
        both = pick(dot(table_ref[...], right), NEAR, 2 * LANES)
        parts += [both[:, 0:LANES], both[:, LANES:]]
    return parts


class Place:
    def __init__(self, sizes):
        self.size_x, self.size_y, _ = sizes
        self.me = lax.axis_index("ctx")
        self.core = lax.rem(self.me, 2)
        self.y = lax.rem(lax.div(self.me, 2), self.size_y)
        self.x = lax.div(self.me, 2 * self.size_y)
        self.partner = self.index(self.x, self.y, 1 - self.core)
        self.y_peers = [
            self.index(self.x, lax.rem(self.y + k, self.size_y), self.core)
            for k in range(1, self.size_y)
        ]
        self.x_peers = [
            self.index(lax.rem(self.x + k, self.size_x), self.y, self.core)
            for k in range(1, self.size_x)
        ]

    def index(self, x, y, core):
        return (x * self.size_y + y) * 2 + core


def remote(source, target, sems, slot, peer):
    return pltpu.make_async_remote_copy(
        src_ref=source, dst_ref=target, send_sem=sems[0].at[slot], recv_sem=sems[1].at[slot],
        device_id=peer, device_id_type=MESH,
    )


def gather(buffer, place, peers, sems, base):
    copies = [
        remote(buffer.at[place], buffer.at[place], sems, base + k, {"ctx": peer})
        for k, peer in enumerate(peers)
    ]
    for copy in copies:
        copy.start()
    return copies


def finish(copies):
    for copy in copies:
        copy.wait()


class Join:
    def __init__(self, place, forward, total_ref, result_ref, log_ref, pair, by_y, by_x, out, sems):
        self.place, self.forward = place, forward
        self.total, self.result, self.log = total_ref, result_ref, log_ref
        self.pair, self.by_y, self.by_x, self.out, self.sems = pair, by_y, by_x, out, sems
        half = total_ref.shape[1] // 2
        self.mine = pl.ds(pl.multiple_of(place.core * half, half), half)
        self.other = pl.ds(pl.multiple_of((1 - place.core) * half, half), half)
        self.span = 4 * NEAR

    def decay(self, steps):
        return jnp.exp(self.log[:, self.mine] * (steps * 1.0))

    def start(self):
        place = self.place
        self.copies = [
            remote(self.total.at[:, self.other], self.pair.at[place.core], self.sems, 0,
                   {"ctx": place.partner})
        ]
        self.copies[0].start()
        self.pair[place.core] = self.total[:, self.mine]

    def along_y(self):
        finish(self.copies)
        first, second = (0, 1) if self.forward else (1, 0)
        chip = self.decay(self.span) * self.pair[first] + self.pair[second]
        self.by_y[self.place.y] = chip
        self.copies = gather(self.by_y, self.place.y, self.place.y_peers, self.sems, 1)

    def walk(self, buffer, count, here, decay):
        before = jnp.zeros(buffer.shape[1:], f32)
        whole = before
        for s in range(count) if self.forward else reversed(range(count)):
            value = buffer[s]
            earlier = (s < here) if self.forward else (s > here)
            before = jnp.where(earlier, decay * before + value, before)
            whole = decay * whole + value
        return before, whole

    def along_x(self):
        finish(self.copies)
        place = self.place
        self.before, whole = self.walk(self.by_y, place.size_y, place.y, self.decay(2 * self.span))
        self.out[1] = self.before
        self.by_x[place.x] = whole
        self.copies = gather(self.by_x, place.x, place.x_peers, self.sems, place.size_y)

    def share(self):
        finish(self.copies)
        place = self.place
        chip = self.decay(2 * self.span)
        before, _ = self.walk(
            self.by_x, place.size_x, place.x, self.decay(2 * self.span * place.size_y)
        )
        inner = place.y if self.forward else place.size_y - 1 - place.y
        for k in range(place.size_y - 1):
            before = jnp.where(k < inner, chip * before, before)
        near = self.out[1] + before
        first = 0 if self.forward else 1
        far = self.decay(self.span) * near + self.pair[first]
        is_first = place.core == first
        self.result[:, self.mine] = jnp.where(is_first, near, far)
        self.out[0] = jnp.where(is_first, far, near)
        self.copies = [
            remote(self.out.at[0], self.result.at[:, self.mine], self.sems,
                   place.size_y + place.size_x - 1, {"ctx": place.partner})
        ]
        self.copies[0].start()

    def end(self):
        finish(self.copies)


def whole_kernel(
    sizes, scale,
    cotangent_in, query_in, key_in, value_in, query_modal_in, key_modal_in,
    filter_ref, decay_ref, residue_ref,
    out0, out1, out2, out3, out4, filter_out,
    query, key, value, query_modal, key_modal, cotangent,
    medium_input, conv, medium_out, grad_conv,
    stage0, stage1, stage2, stage3, stage4,
    end_states, start_states, own_total, own_adjoint, entering, arriving, log_rows,
    pair_f, y_f, x_f, o_f, pair_b, y_b, x_b, o_b,
    forward_row, adjoint_row, table, wide, left, sums, core_sums, y_sums, x_sums,
    load_sem, cot_send, cot_recv, tail_send, tail_recv, head_send, head_recv,
    join_send, join_recv, back_send, back_recv, sum_send, sum_recv,
    out_send, out_recv, own_sem,
):
    place = Place(sizes)
    me, z = place.me, lax.axis_index("ch")
    size_z = lax.axis_size("ch")
    devices = lax.axis_size("ctx")
    row_count, channels = query.shape
    blocks = row_count // NEAR
    tiles = channels // LANES
    modes = own_total.shape[0]
    part = channels // CHUNKS
    following = lax.rem(me + 1, devices)
    previous = lax.rem(me + devices - 1, devices)

    def columns(chunk):
        return pl.ds(chunk * part, part)

    loads = [
        pltpu.make_async_copy(source, target, load_sem.at[n])
        for n, (source, target) in enumerate(
            [(key_in, key), (value_in, value), (query_in, query), (key_modal_in, key_modal),
             (query_modal_in, query_modal)]
        )
    ]
    for copy in loads:
        copy.start()

    z_peers = [lax.rem(z + k, size_z) for k in range(1, size_z)]
    barrier = pltpu.get_barrier_semaphore()
    for peer in z_peers:
        pl.semaphore_signal(barrier, inc=1, device_id={"ch": peer}, device_id_type=MESH)
    ring = [place.partner] + place.y_peers + place.x_peers + [following, previous]
    for peer in ring:
        pl.semaphore_signal(barrier, inc=1, device_id={"ctx": peer}, device_id_type=MESH)
    pl.semaphore_wait(barrier, len(z_peers) + len(ring))

    own_rows = pl.ds(pl.multiple_of(z * NEAR, NEAR), NEAR)
    own_columns = pl.ds(pl.multiple_of(z * channels, channels), channels)

    cot_copies = []
    for chunk in range(CHUNKS):
        for k, peer in enumerate(z_peers):
            source = pl.ds(pl.multiple_of(peer * channels + chunk * part, part), part)
            copy = remote(
                cotangent_in.at[:, source], cotangent.at[own_rows, columns(chunk)],
                (cot_send.at[k], cot_recv.at[k]), chunk, {"ch": peer},
            )
            copy.start()
            cot_copies.append(copy)
    cot_own = pltpu.make_async_copy(
        cotangent_in.at[:, own_columns], cotangent.at[own_rows], own_sem.at[5]
    )
    cot_own.start()

    loads[0].wait()
    loads[1].wait()
    last = slice(row_count - TAPS, row_count)
    medium_input[row_count:] = product(key[last], value[last])
    tail_copies = [
        remote(
            medium_input.at[pl.ds(row_count, TAPS), columns(c)],
            medium_input.at[pl.ds(0, TAPS), columns(c)],
            (tail_send, tail_recv), c, {"ctx": following},
        )
        for c in range(CHUNKS)
    ]
    for copy in tail_copies:
        copy.start()

    taps_in = filter_ref[...]
    turn = jnp.where(
        iota((TAPS, 2 * TAPS), 0) + iota((TAPS, 2 * TAPS), 1) == TAPS, 1.0, 0.0
    ).astype(bf16)
    forward_row[...] = dot(taps_in, turn)
    adjoint_row[:, 0:TAPS] = taps_in.astype(f32)
    adjoint_row[:, TAPS:] = jnp.zeros(taps_in.shape, f32)
    wide[NEAR + 3 * modes :] = jnp.zeros((NEAR - 3 * modes, wide.shape[1]), bf16)
    spread = jnp.where(
        lax.shift_right_logical(ramp(0), 4) == lax.shift_right_logical(ramp(1), 4), 1.0, 0.0
    )
    own_mode = jnp.bitwise_and(iota((modes, LANES), 1), modes - 1) == iota((modes, LANES), 0)

    def lanes_of(tile):
        return pl.ds(pl.multiple_of(tile * LANES, LANES), LANES)

    @pl.loop(0, tiles)
    def _(tile):
        kept = jnp.where(own_mode, decay_ref[pl.ds(tile, 1)], 0.0)
        log_rows[:, lanes_of(tile)] = jnp.log(
            jnp.dot(kept, spread, precision=highest, preferred_element_type=f32)
        )

    loads[2].wait()
    loads[3].wait()
    early = slice(0, row_count - TAPS)

    for chunk in range(CHUNKS):
        tail_copies[chunk].wait_recv()

        @pl.when(me == 0)
        def _():
            medium_input[0:TAPS, columns(chunk)] = jnp.zeros((TAPS, part), bf16)

        @pl.loop(chunk * tiles // CHUNKS, (chunk + 1) * tiles // CHUNKS)
        def _(tile):
            lanes = lanes_of(tile)
            medium_input[TAPS:row_count, lanes] = product(key[early, lanes], value[early, lanes])
            fill_medium_table(table, forward_row, tile)
            inputs = []
            for pair in range(blocks // 2):
                both = medium_pair(table, medium_input, lanes, pair)
                for half in range(2):
                    rows = block_rows(2 * pair + half)
                    part_conv = both[:, LANES * half : LANES * (half + 1)]
                    conv[rows, lanes] = part_conv
                    out = (query[rows, lanes].astype(f32) * part_conv).astype(bf16)
                    medium_out[rows, lanes] = out
                    inputs.append(product(key_modal[rows, lanes], out))
            log_row = jnp.log(decay_ref[pl.ds(tile, 1)])
            weight = jnp.exp(log_row * (NEAR - 1 - ramp(0)).astype(f32))
            states = block_states(weight, jnp.concatenate(inputs, axis=1))
            step = jnp.exp(log_rows[:, lanes] * NEAR)
            total = jnp.zeros((modes, LANES), f32)
            for b in range(blocks):
                state = states[:, LANES * b : LANES * (b + 1)]
                end_states[b, :, lanes] = state
                total = step * total + state
            own_total[:, lanes] = total

    forward = Join(place, True, own_total, entering, log_rows, pair_f, y_f, x_f, o_f,
                   (join_send, join_recv))
    backward = Join(place, False, own_adjoint, arriving, log_rows, pair_b, y_b, x_b, o_b,
                    (back_send, back_recv))
    forward.start()
    cot_own.wait()
    loads[4].wait()
    forward.along_y()

    def adjoint_states(chunk):
        for copy in cot_copies[(size_z - 1) * chunk : (size_z - 1) * (chunk + 1)]:
            copy.wait_recv()

        @pl.loop(chunk * tiles // CHUNKS, (chunk + 1) * tiles // CHUNKS)
        def _(tile):
            lanes = lanes_of(tile)
            grads = jnp.concatenate(
                [product(cotangent[block_rows(b), lanes], query_modal[block_rows(b), lanes])
                 for b in range(blocks)],
                axis=1,
            )
            log_row = jnp.log(decay_ref[pl.ds(tile, 1)])
            states = block_states(jnp.exp(log_row * ramp(0).astype(f32)), grads)
            step = jnp.exp(log_rows[:, lanes] * NEAR)
            total = jnp.zeros((modes, LANES), f32)
            for b in reversed(range(blocks)):
                state = states[:, LANES * b : LANES * (b + 1)]
                start_states[b, :, lanes] = state
                total = step * total + state
            own_adjoint[:, lanes] = total

    adjoint_states(0)
    adjoint_states(1)
    forward.along_x()
    adjoint_states(2)
    adjoint_states(3)
    forward.share()
    backward.start()
    forward.end()

    out_copies, own_copies = [], []

    def send_home(n, stage, out, chunk):
        for k, peer in enumerate(z_peers):
            rows = pl.ds(pl.multiple_of(peer * NEAR, NEAR), NEAR)
            target = pl.ds(pl.multiple_of(z * channels + chunk * part, part), part)
            copy = remote(
                stage.at[rows, columns(chunk)], out.at[:, target],
                (out_send.at[n, k], out_recv.at[n, k]), chunk, {"ch": peer},
            )
            copy.start()
            out_copies.append(copy)
        if chunk == CHUNKS - 1:
            copy = pltpu.make_async_copy(
                stage.at[own_rows], out.at[:, own_columns], own_sem.at[n]
            )
            copy.start()
            own_copies.append(copy)

    for chunk in range(CHUNKS):

        @pl.loop(chunk * tiles // CHUNKS, (chunk + 1) * tiles // CHUNKS)
        def _(tile):
            lanes = lanes_of(tile)
            log_row = jnp.log(decay_ref[pl.ds(tile, 1)])
            fill_modal_table(table, log_row, residue_ref[pl.ds(tile, 1)], modes, False)
            step = jnp.exp(log_rows[:, lanes] * NEAR)
            carried = entering[:, lanes]
            befores = []
            for b in range(blocks):
                wide[0:NEAR, LANES * b : LANES * (b + 1)] = product(
                    key_modal[block_rows(b), lanes], medium_out[block_rows(b), lanes]
                )
                befores.append(carried)
                carried = step * carried + end_states[b, :, lanes]
            parts = modal_blocks(table, wide, jnp.concatenate(befores, axis=1))
            for b in range(blocks):
                rows = block_rows(b)
                stage3[rows, lanes] = (cotangent[rows, lanes].astype(f32) * parts[b]).astype(bf16)

        send_home(3, stage3, out3, chunk)
        if chunk == 0:
            backward.along_y()
        if chunk == 1:
            backward.along_x()
        if chunk == 2:
            backward.share()
    backward.end()

    head_copies = []
    for chunk in range(CHUNKS):

        @pl.loop(chunk * tiles // CHUNKS, (chunk + 1) * tiles // CHUNKS)
        def _(tile):
            lanes = lanes_of(tile)
            log_row = jnp.log(decay_ref[pl.ds(tile, 1)])
            fill_modal_table(table, log_row, residue_ref[pl.ds(tile, 1)], modes, True)
            step = jnp.exp(log_rows[:, lanes] * NEAR)
            carried = arriving[:, lanes]
            nexts = [carried] * blocks
            for b in reversed(range(blocks)):
                wide[0:NEAR, LANES * b : LANES * (b + 1)] = product(
                    cotangent[block_rows(b), lanes], query_modal[block_rows(b), lanes]
                )
                nexts[b] = carried
                carried = step * carried + start_states[b, :, lanes]
            parts = modal_blocks(table, wide, jnp.concatenate(nexts, axis=1))
            for b in range(blocks):
                rows = block_rows(b)
                stage4[rows, lanes] = (parts[b] * medium_out[rows, lanes].astype(f32)).astype(bf16)
                grad_out = parts[b] * key_modal[rows, lanes].astype(f32)
                stage0[rows, lanes] = (grad_out * conv[rows, lanes]).astype(bf16)
                grad_conv[rows, lanes] = (grad_out * query[rows, lanes].astype(f32)).astype(bf16)

        copy = remote(
            grad_conv.at[pl.ds(0, TAPS), columns(chunk)],
            grad_conv.at[pl.ds(row_count, TAPS), columns(chunk)],
            (head_send, head_recv), chunk, {"ctx": previous},
        )
        copy.start()
        head_copies.append(copy)
        send_home(4, stage4, out4, chunk)
        send_home(0, stage0, out0, chunk)

    flip = jnp.where(ramp(0) + ramp(1) == NEAR - 1, 1.0, 0.0)

    @pl.loop(0, tiles)
    def _(tile):
        lanes = lanes_of(tile)
        grads = jnp.concatenate([grad_conv[block_rows(b), lanes] for b in range(blocks)], axis=1)
        flipped = dot(flip.astype(bf16), grads)
        group = lane_group(NEAR, blocks * LANES)
        for g in range(TILE_GROUPS):
            left[block_rows(g)] = jnp.where(group == g, flipped, 0.0).astype(bf16)
        right = jnp.concatenate(
            [medium_input[NEAR * b : NEAR * (b + 2), lanes] for b in range(blocks)], axis=1
        )
        products = lax.dot_general(
            left[...], right, (((1,), (1,)), ((), ())), preferred_element_type=f32
        )
        rows = []
        for g in range(TILE_GROUPS):
            turned = pltpu.roll(products[block_rows(g)], 0, 1, stride=1, stride_axis=0)
            rows.append(jnp.sum(turned[:, NEAR:], axis=0, keepdims=True))
        sums[pl.ds(pl.multiple_of(tile * TILE_GROUPS, TILE_GROUPS), TILE_GROUPS)] = (
            jnp.concatenate(rows, axis=0)
        )

    core_sums[place.core] = sums[...]
    sum_sems = (sum_send, sum_recv)
    sum_copies = gather(core_sums, place.core, [place.partner], sum_sems, 0)

    for chunk in range(CHUNKS):
        head_copies[chunk].wait_recv()

        @pl.when(me == devices - 1)
        def _():
            grad_conv[row_count:, columns(chunk)] = jnp.zeros((TAPS, part), bf16)

        @pl.loop(chunk * tiles // CHUNKS, (chunk + 1) * tiles // CHUNKS)
        def _(tile):
            lanes = lanes_of(tile)
            fill_medium_table(table, adjoint_row, tile)
            for pair in range(blocks // 2):
                both = medium_pair(table, grad_conv, lanes, pair)
                for half in range(2):
                    rows = block_rows(2 * pair + half)
                    grad_input = both[:, LANES * half : LANES * (half + 1)]
                    stage1[rows, lanes] = (grad_input * value[rows, lanes].astype(f32)).astype(bf16)
                    stage2[rows, lanes] = (grad_input * key[rows, lanes].astype(f32)).astype(bf16)

        send_home(1, stage1, out1, chunk)
        send_home(2, stage2, out2, chunk)
        if chunk == 0:
            finish(sum_copies)
            y_sums[place.y] = core_sums[0] + core_sums[1]
            sum_copies = gather(y_sums, place.y, place.y_peers, sum_sems, 1)
        if chunk == 1:
            finish(sum_copies)
            x_sums[place.x] = sum(y_sums[s] for s in range(1, place.size_y)) + y_sums[0]
            sum_copies = gather(x_sums, place.x, place.x_peers, sum_sems, place.size_y)
    finish(sum_copies)
    summed = sum(x_sums[s] for s in range(1, place.size_x)) + x_sums[0]
    filter_out[...] = (
        jnp.dot(summed, flip, precision=highest, preferred_element_type=f32) * scale
    )

    for copy in cot_copies + tail_copies + head_copies:
        copy.wait_send()
    for copy in own_copies:
        copy.wait()
    finish(out_copies)


def on_device(
    sizes, grad_out, query_medium, key_medium, value_medium, query_modal, key_modal,
    medium_filter, modal_decay, modal_residue,
):
    row_count, channels = query_medium.shape
    blocks = row_count // NEAR
    groups, modes = modal_decay.shape
    devices = lax.axis_size("ctx")
    size_z = lax.axis_size("ch")
    size_x, size_y, _ = sizes
    output = jax.ShapeDtypeStruct(grad_out.shape, bf16)
    filter_output = jax.ShapeDtypeStruct((groups, TAPS), f32)
    scale = 1.0 / math.sqrt(row_count * devices * GS)
    decay_rows = modal_decay.reshape(groups * modes // LANES, LANES)
    residue_rows = modal_residue.reshape(groups * modes // LANES, LANES)
    data = pltpu.VMEM((row_count, channels), bf16)
    longer = pltpu.VMEM((row_count + TAPS, channels), bf16)
    states = pltpu.VMEM((blocks, modes, channels), f32)
    state = pltpu.VMEM((modes, channels), f32)
    half = (modes, channels // 2)
    joins = [pltpu.VMEM((n,) + half, f32) for n in (2, size_y, size_x, 2)]
    dma = pltpu.SemaphoreType.DMA
    square = (groups, TAPS)
    whole = pl.BlockSpec(memory_space=pl.ANY)
    local = pl.BlockSpec(memory_space=pltpu.VMEM)
    outs = pl.pallas_call(
        lambda *refs: whole_kernel(sizes, scale, *refs),
        in_specs=[whole] * 6 + [local] * 3,
        out_shape=(output,) * 5 + (filter_output,),
        out_specs=(whole,) * 5 + (local,),
        scratch_shapes=[data] * 6
        + [longer, pltpu.VMEM((row_count, channels), f32), data, longer]
        + [data] * 5
        + [states] * 2 + [state] * 5
        + joins * 2
        + [pltpu.VMEM((groups, 2 * TAPS), f32)] * 2
        + [pltpu.VMEM((TILE_GROUPS * NEAR, 2 * NEAR), bf16),
           pltpu.VMEM((2 * NEAR, blocks * LANES), bf16),
           pltpu.VMEM((TILE_GROUPS * NEAR, blocks * LANES), bf16)]
        + [pltpu.VMEM(square, f32)]
        + [pltpu.VMEM((n,) + square, f32) for n in (2, size_y, size_x)]
        + [dma((5,))] + [dma((size_z - 1, CHUNKS))] * 2 + [dma((CHUNKS,))] * 4
        + [dma((size_x + size_y,))] * 4 + [dma((size_x + size_y,))] * 2
        + [dma((5, size_z - 1, CHUNKS))] * 2 + [dma((6,))],
        compiler_params=pltpu.CompilerParams(
            collective_id=0, has_side_effects=True, vmem_limit_bytes=60 * 1024 * 1024
        ),
    )(
        grad_out, query_medium, key_medium, value_medium, query_modal, key_modal,
        medium_filter, decay_rows, residue_rows,
    )
    return tuple(outs)


def solution(mesh):
    count = mesh.shape["ctx"] // 2
    side = math.isqrt(count)
    sizes = (side, count // side, 2)

    def body(*args):
        return on_device(sizes, *args)

    rows = P(("ctx", "ch"), None)
    groups = P("ch", None)
    return jax.shard_map(
        body,
        mesh=mesh,
        in_specs=(rows,) + (P("ctx", "ch"),) * 5 + (groups,) * 3,
        out_specs=(rows,) * 5 + (groups,),
        check_vma=False,
    )
```

```python
import math

import jax
import jax.numpy as jnp
from jax import lax
from jax.experimental import pallas as pl
from jax.experimental.pallas import tpu as pltpu
from jax.sharding import PartitionSpec as P

GS = 16
TAPS = 128
NEAR = 128
LANES = 128
TILE_GROUPS = LANES // GS
CHUNKS = 4
MESH = pl.DeviceIdType.MESH

f32 = jnp.float32
bf16 = jnp.bfloat16
highest = lax.Precision.HIGHEST


def dot(a, b):
    return jnp.dot(a, b, preferred_element_type=f32)


def iota(shape, axis):
    return lax.broadcasted_iota(jnp.int32, shape, axis)


def ramp(axis):
    return iota((NEAR, LANES), axis)


def lane_group(rows, columns):
    lane = iota((rows, columns), 1)
    return jnp.bitwise_and(lax.shift_right_logical(lane, 4), TILE_GROUPS - 1)


def pick(stacked, rows, columns):
    group = lane_group(rows, columns)
    kept = stacked[0:rows]
    for g in range(1, TILE_GROUPS):
        kept = jnp.where(group == g, stacked[g * rows : (g + 1) * rows], kept)
    return kept


def skewed(row, height):
    wide = jnp.broadcast_to(row, (height, row.shape[1]))
    return pltpu.roll(wide, 0, 1, stride=1, stride_axis=0)


def split(value):
    high = value.astype(bf16)
    return high, (value - high.astype(f32)).astype(bf16)


def product(a, b):
    return (a.astype(f32) * b.astype(f32)).astype(bf16)


def block_rows(b):
    return slice(NEAR * b, NEAR * (b + 1))


def block_states(weight, data):
    high, low = split(weight.T)
    left = jnp.concatenate([high, low], axis=1)
    right = jnp.concatenate([data, data], axis=0)
    return pick(dot(left, right), weight.shape[1] // TILE_GROUPS, data.shape[1])


def fill_medium_table(table_ref, row_ref, tile):
    rows = row_ref[pl.ds(pl.multiple_of(tile * TILE_GROUPS, TILE_GROUPS), TILE_GROUPS)]
    for g in range(TILE_GROUPS):
        table_ref[block_rows(g)] = skewed(rows[g : g + 1], NEAR).astype(bf16)


def medium_pair(table_ref, data_ref, lanes, pair):
    low = 2 * pair * NEAR
    right = jnp.concatenate(
        [data_ref[low : low + 2 * NEAR, lanes], data_ref[low + NEAR : low + 3 * NEAR, lanes]],
        axis=1,
    )
    return pick(dot(table_ref[...], right), NEAR, 2 * LANES)


def fill_modal_table(table_ref, log_row, residue_row, modes, adjoint):
    row, lane = ramp(0), ramp(1)
    lag = row if adjoint else jnp.bitwise_and(NEAR - row, NEAR - 1)
    terms = residue_row * jnp.exp(log_row * lag.astype(f32))
    member = jnp.where(lane_group(TILE_GROUPS, LANES) == iota((TILE_GROUPS, LANES), 0), 1.0, 0.0)
    taps = lax.dot_general(
        member, terms, (((1,), (1,)), ((), ())), precision=highest, preferred_element_type=f32
    )
    small = iota((TILE_GROUPS, LANES), 1)

    def three(value):
        turned = pltpu.roll(
            jnp.broadcast_to(value, (TILE_GROUPS, LANES)), 0, 1, stride=modes, stride_axis=0
        )
        again, third = pltpu.roll(turned, modes, 1), pltpu.roll(turned, 2 * modes, 1)
        return jnp.where(small < modes, turned, jnp.where(small < 2 * modes, again, third))

    logs, residues = three(log_row), jnp.where(small < 3 * modes, three(residue_row), 0.0)
    near = row <= lane if adjoint else lane <= row
    far_lag = ((NEAR - row) if adjoint else (row + 1)).astype(f32)
    for g in range(TILE_GROUPS):
        q = (TILE_GROUPS - g) % TILE_GROUPS
        table_ref[block_rows(g), 0:LANES] = jnp.where(
            near, skewed(taps[g : g + 1], NEAR), 0.0
        ).astype(bf16)
        far = residues[q : q + 1] * jnp.exp(logs[q : q + 1] * far_lag)
        high = far.astype(bf16).astype(f32)
        table_ref[block_rows(g), LANES:] = jnp.where(
            lane < 2 * modes, high, far - high
        ).astype(bf16)


def modal_blocks(table_ref, data_ref, states):
    high, low = split(states)
    modes = states.shape[0]
    data_ref[NEAR : NEAR + modes] = high
    data_ref[NEAR + modes : NEAR + 2 * modes] = low
    data_ref[NEAR + 2 * modes : NEAR + 3 * modes] = high
    parts = []
    for pair in range(data_ref.shape[1] // (2 * LANES)):
        right = data_ref[:, 2 * LANES * pair : 2 * LANES * (pair + 1)]
        both = pick(dot(table_ref[...], right), NEAR, 2 * LANES)
        parts += [both[:, 0:LANES], both[:, LANES:]]
    return parts


class Place:
    def __init__(self, sizes):
        self.size_x, self.size_y, _ = sizes
        self.me = lax.axis_index("ctx")
        self.core = lax.rem(self.me, 2)
        self.y = lax.rem(lax.div(self.me, 2), self.size_y)
        self.x = lax.div(self.me, 2 * self.size_y)
        self.partner = self.index(self.x, self.y, 1 - self.core)
        self.y_peers = [
            self.index(self.x, lax.rem(self.y + k, self.size_y), self.core)
            for k in range(1, self.size_y)
        ]
        self.x_peers = [
            self.index(lax.rem(self.x + k, self.size_x), self.y, self.core)
            for k in range(1, self.size_x)
        ]

    def index(self, x, y, core):
        return (x * self.size_y + y) * 2 + core


def remote(source, target, sems, slot, peer):
    return pltpu.make_async_remote_copy(
        src_ref=source, dst_ref=target, send_sem=sems[0].at[slot], recv_sem=sems[1].at[slot],
        device_id=peer, device_id_type=MESH,
    )


def gather(buffer, place, peers, sems, base):
    copies = [
        remote(buffer.at[place], buffer.at[place], sems, base + k, {"ctx": peer})
        for k, peer in enumerate(peers)
    ]
    for copy in copies:
        copy.start()
    return copies


def finish(copies):
    for copy in copies:
        copy.wait()


class Join:
    def __init__(
        self, place, forward, low, width, total_ref, result_ref, log_ref, pair, by_y, by_x, out, sems
    ):
        self.place, self.forward = place, forward
        self.total, self.result, self.log = total_ref, result_ref, log_ref
        self.pair, self.by_y, self.by_x, self.out, self.sems = pair, by_y, by_x, out, sems
        half = width // 2
        self.mine = pl.ds(pl.multiple_of(low + place.core * half, half), half)
        self.other = pl.ds(pl.multiple_of(low + (1 - place.core) * half, half), half)
        self.span = 4 * NEAR

    def decay(self, steps):
        return jnp.exp(self.log[:, self.mine] * (steps * 1.0))

    def start(self):
        place = self.place
        self.copies = [
            remote(self.total.at[:, self.other], self.pair.at[place.core], self.sems, 0,
                   {"ctx": place.partner})
        ]
        self.copies[0].start()
        self.pair[place.core] = self.total[:, self.mine]

    def along_y(self):
        finish(self.copies)
        first, second = (0, 1) if self.forward else (1, 0)
        chip = self.decay(self.span) * self.pair[first] + self.pair[second]
        self.by_y[self.place.y] = chip
        self.copies = gather(self.by_y, self.place.y, self.place.y_peers, self.sems, 1)

    def walk(self, buffer, count, here, decay):
        before = jnp.zeros(buffer.shape[1:], f32)
        whole = before
        for s in range(count) if self.forward else reversed(range(count)):
            value = buffer[s]
            earlier = (s < here) if self.forward else (s > here)
            before = jnp.where(earlier, decay * before + value, before)
            whole = decay * whole + value
        return before, whole

    def along_x(self):
        finish(self.copies)
        place = self.place
        self.before, whole = self.walk(self.by_y, place.size_y, place.y, self.decay(2 * self.span))
        self.out[1] = self.before
        self.by_x[place.x] = whole
        self.copies = gather(self.by_x, place.x, place.x_peers, self.sems, place.size_y)

    def share(self):
        finish(self.copies)
        place = self.place
        chip = self.decay(2 * self.span)
        before, _ = self.walk(
            self.by_x, place.size_x, place.x, self.decay(2 * self.span * place.size_y)
        )
        inner = place.y if self.forward else place.size_y - 1 - place.y
        for k in range(place.size_y - 1):
            before = jnp.where(k < inner, chip * before, before)
        near = self.out[1] + before
        first = 0 if self.forward else 1
        far = self.decay(self.span) * near + self.pair[first]
        is_first = place.core == first
        self.result[:, self.mine] = jnp.where(is_first, near, far)
        self.out[0] = jnp.where(is_first, far, near)
        self.copies = [
            remote(self.out.at[0], self.result.at[:, self.mine], self.sems,
                   place.size_y + place.size_x - 1, {"ctx": place.partner})
        ]
        self.copies[0].start()

    def end(self):
        finish(self.copies)


def whole_kernel(
    sizes, scale,
    cotangent_in, query_in, key_in, value_in, query_modal_in, key_modal_in,
    filter_ref, decay_ref, residue_ref,
    out0, out1, out2, out3, out4, filter_out,
    query, key, value, query_modal, key_modal, cotangent,
    medium_input, conv, medium_out, grad_conv,
    stage0, stage1, stage2, stage3, stage4,
    end_states, start_states, own_total, own_adjoint, entering, arriving, log_rows,
    pair_f, y_f, x_f, o_f, pair_s, y_s, x_s, o_s, pair_b, y_b, x_b, o_b,
    decay_rows, residue_rows, forward_row, adjoint_row, table, wide, left, sums, core_sums, y_sums, x_sums,
    load_sem, cot_send, cot_recv, tail_send, tail_recv, head_send, head_recv,
    join_send, join_recv, join2_send, join2_recv, back_send, back_recv, sum_send, sum_recv,
    out_send, out_recv, own_sem,
):
    place = Place(sizes)
    me, z = place.me, lax.axis_index("ch")
    size_z = lax.axis_size("ch")
    devices = lax.axis_size("ctx")
    row_count, channels = query.shape
    blocks = row_count // NEAR
    tiles = channels // LANES
    modes, groups = decay_ref.shape
    part = channels // CHUNKS
    following = lax.rem(me + 1, devices)
    previous = lax.rem(me + devices - 1, devices)

    def columns(chunk):
        return pl.ds(chunk * part, part)

    loads = [
        pltpu.make_async_copy(source, target, load_sem.at[n])
        for n, (source, target) in enumerate(
            [(key_in, key), (value_in, value), (query_in, query), (key_modal_in, key_modal),
             (query_modal_in, query_modal)]
        )
    ]
    for copy in loads:
        copy.start()

    z_peers = [lax.rem(z + k, size_z) for k in range(1, size_z)]
    barrier = pltpu.get_barrier_semaphore()
    for peer in z_peers:
        pl.semaphore_signal(barrier, inc=1, device_id={"ch": peer}, device_id_type=MESH)
    ring = [place.partner] + place.y_peers + place.x_peers + [following, previous]
    for peer in ring:
        pl.semaphore_signal(barrier, inc=1, device_id={"ctx": peer}, device_id_type=MESH)
    pl.semaphore_wait(barrier, len(z_peers) + len(ring))

    own_rows = pl.ds(pl.multiple_of(z * NEAR, NEAR), NEAR)
    own_columns = pl.ds(pl.multiple_of(z * channels, channels), channels)

    cot_copies = []
    for chunk in range(CHUNKS):
        for k, peer in enumerate(z_peers):
            source = pl.ds(pl.multiple_of(peer * channels + chunk * part, part), part)
            copy = remote(
                cotangent_in.at[:, source], cotangent.at[own_rows, columns(chunk)],
                (cot_send.at[k], cot_recv.at[k]), chunk, {"ch": peer},
            )
            copy.start()
            cot_copies.append(copy)
    cot_own = pltpu.make_async_copy(
        cotangent_in.at[:, own_columns], cotangent.at[own_rows], own_sem.at[5]
    )
    cot_own.start()

    loads[0].wait()
    loads[1].wait()
    last = slice(row_count - TAPS, row_count)
    medium_input[row_count:] = product(key[last], value[last])
    tail_copies = [
        remote(
            medium_input.at[pl.ds(row_count, TAPS), columns(c)],
            medium_input.at[pl.ds(0, TAPS), columns(c)],
            (tail_send, tail_recv), c, {"ctx": following},
        )
        for c in range(CHUNKS)
    ]
    for copy in tail_copies:
        copy.start()

    taps_in = filter_ref[...]
    turn = jnp.where(
        iota((TAPS, 2 * TAPS), 0) + iota((TAPS, 2 * TAPS), 1) == TAPS, 1.0, 0.0
    ).astype(bf16)
    forward_row[...] = dot(taps_in, turn)
    adjoint_row[:, 0:TAPS] = taps_in.astype(f32)
    adjoint_row[:, TAPS:] = jnp.zeros(taps_in.shape, f32)
    wide[NEAR + 3 * modes :] = jnp.zeros((NEAR - 3 * modes, wide.shape[1]), bf16)
    own_mode = jnp.bitwise_and(iota((modes, LANES), 1), modes - 1) == iota((modes, LANES), 0)

    def lanes_of(tile):
        return pl.ds(pl.multiple_of(tile * LANES, LANES), LANES)

    @pl.loop(0, tiles)
    def _(tile):
        spread = jnp.where(
            iota((groups, LANES), 0)
            == tile * TILE_GROUPS + lax.shift_right_logical(iota((groups, LANES), 1), 4),
            1.0, 0.0,
        )

        def per_channel(ref):
            return jnp.dot(ref[...], spread, precision=highest, preferred_element_type=f32)

        def per_mode(value):
            return jnp.sum(jnp.where(own_mode, value, 0.0), axis=0, keepdims=True)

        decay = per_channel(decay_ref)
        log_rows[:, lanes_of(tile)] = jnp.log(decay)
        decay_rows[pl.ds(tile, 1)] = per_mode(decay)
        residue_rows[pl.ds(tile, 1)] = per_mode(per_channel(residue_ref))

    loads[2].wait()
    loads[3].wait()
    early = slice(0, row_count - TAPS)

    def medium_forward(chunk):
        tail_copies[chunk].wait_recv()

        @pl.when(me == 0)
        def _():
            medium_input[0:TAPS, columns(chunk)] = jnp.zeros((TAPS, part), bf16)

        @pl.loop(chunk * tiles // CHUNKS, (chunk + 1) * tiles // CHUNKS)
        def _(tile):
            lanes = lanes_of(tile)
            medium_input[TAPS:row_count, lanes] = product(key[early, lanes], value[early, lanes])
            fill_medium_table(table, forward_row, tile)
            inputs = []
            for pair in range(blocks // 2):
                both = medium_pair(table, medium_input, lanes, pair)
                for half in range(2):
                    rows = block_rows(2 * pair + half)
                    part_conv = both[:, LANES * half : LANES * (half + 1)]
                    conv[rows, lanes] = part_conv
                    out = (query[rows, lanes].astype(f32) * part_conv).astype(bf16)
                    medium_out[rows, lanes] = out
                    inputs.append(product(key_modal[rows, lanes], out))
            log_row = jnp.log(decay_rows[pl.ds(tile, 1)])
            weight = jnp.exp(log_row * (NEAR - 1 - ramp(0)).astype(f32))
            states = block_states(weight, jnp.concatenate(inputs, axis=1))
            step = jnp.exp(log_rows[:, lanes] * NEAR)
            total = jnp.zeros((modes, LANES), f32)
            for b in range(blocks):
                state = states[:, LANES * b : LANES * (b + 1)]
                end_states[b, :, lanes] = state
                total = step * total + state
            own_total[:, lanes] = total

    def adjoint_states(chunk):
        for copy in cot_copies[(size_z - 1) * chunk : (size_z - 1) * (chunk + 1)]:
            copy.wait_recv()

        @pl.loop(chunk * tiles // CHUNKS, (chunk + 1) * tiles // CHUNKS)
        def _(tile):
            lanes = lanes_of(tile)
            grads = jnp.concatenate(
                [product(cotangent[block_rows(b), lanes], query_modal[block_rows(b), lanes])
                 for b in range(blocks)],
                axis=1,
            )
            log_row = jnp.log(decay_rows[pl.ds(tile, 1)])
            states = block_states(jnp.exp(log_row * ramp(0).astype(f32)), grads)
            step = jnp.exp(log_rows[:, lanes] * NEAR)
            total = jnp.zeros((modes, LANES), f32)
            for b in reversed(range(blocks)):
                state = states[:, LANES * b : LANES * (b + 1)]
                start_states[b, :, lanes] = state
                total = step * total + state
            own_adjoint[:, lanes] = total

    out_copies, own_copies = [], []

    def send_home(n, stage, out, chunk):
        for k, peer in enumerate(z_peers):
            rows = pl.ds(pl.multiple_of(peer * NEAR, NEAR), NEAR)
            target = pl.ds(pl.multiple_of(z * channels + chunk * part, part), part)
            copy = remote(
                stage.at[rows, columns(chunk)], out.at[:, target],
                (out_send.at[n, k], out_recv.at[n, k]), chunk, {"ch": peer},
            )
            copy.start()
            out_copies.append(copy)
        if chunk == CHUNKS - 1:
            copy = pltpu.make_async_copy(
                stage.at[own_rows], out.at[:, own_columns], own_sem.at[n]
            )
            copy.start()
            own_copies.append(copy)

    def modal_forward(chunk):
        @pl.loop(chunk * tiles // CHUNKS, (chunk + 1) * tiles // CHUNKS)
        def _(tile):
            lanes = lanes_of(tile)
            log_row = jnp.log(decay_rows[pl.ds(tile, 1)])
            fill_modal_table(table, log_row, residue_rows[pl.ds(tile, 1)], modes, False)
            step = jnp.exp(log_rows[:, lanes] * NEAR)
            carried = entering[:, lanes]
            befores = []
            for b in range(blocks):
                wide[0:NEAR, LANES * b : LANES * (b + 1)] = product(
                    key_modal[block_rows(b), lanes], medium_out[block_rows(b), lanes]
                )
                befores.append(carried)
                carried = step * carried + end_states[b, :, lanes]
            parts = modal_blocks(table, wide, jnp.concatenate(befores, axis=1))
            for b in range(blocks):
                rows = block_rows(b)
                stage3[rows, lanes] = (cotangent[rows, lanes].astype(f32) * parts[b]).astype(bf16)

        send_home(3, stage3, out3, chunk)

    half = channels // 2
    first = Join(place, True, 0, half, own_total, entering, log_rows, pair_f, y_f, x_f, o_f,
                 (join_send, join_recv))
    second = Join(place, True, half, half, own_total, entering, log_rows, pair_s, y_s, x_s, o_s,
                  (join2_send, join2_recv))
    backward = Join(place, False, 0, channels, own_adjoint, arriving, log_rows,
                    pair_b, y_b, x_b, o_b, (back_send, back_recv))
    medium_forward(0)
    medium_forward(1)
    first.start()
    medium_forward(2)
    first.along_y()
    medium_forward(3)
    second.start()
    first.along_x()
    cot_own.wait()
    loads[4].wait()
    adjoint_states(0)
    second.along_y()
    first.share()
    adjoint_states(1)
    second.along_x()
    first.end()
    modal_forward(0)
    second.share()
    modal_forward(1)
    second.end()
    adjoint_states(2)
    adjoint_states(3)
    backward.start()
    modal_forward(2)
    backward.along_y()
    modal_forward(3)
    backward.along_x()
    backward.share()
    backward.end()

    head_copies = []
    for chunk in range(CHUNKS):

        @pl.loop(chunk * tiles // CHUNKS, (chunk + 1) * tiles // CHUNKS)
        def _(tile):
            lanes = lanes_of(tile)
            log_row = jnp.log(decay_rows[pl.ds(tile, 1)])
            fill_modal_table(table, log_row, residue_rows[pl.ds(tile, 1)], modes, True)
            step = jnp.exp(log_rows[:, lanes] * NEAR)
            carried = arriving[:, lanes]
            nexts = [carried] * blocks
            for b in reversed(range(blocks)):
                wide[0:NEAR, LANES * b : LANES * (b + 1)] = product(
                    cotangent[block_rows(b), lanes], query_modal[block_rows(b), lanes]
                )
                nexts[b] = carried
                carried = step * carried + start_states[b, :, lanes]
            parts = modal_blocks(table, wide, jnp.concatenate(nexts, axis=1))
            for b in range(blocks):
                rows = block_rows(b)
                stage4[rows, lanes] = (parts[b] * medium_out[rows, lanes].astype(f32)).astype(bf16)
                grad_out = parts[b] * key_modal[rows, lanes].astype(f32)
                stage0[rows, lanes] = (grad_out * conv[rows, lanes]).astype(bf16)
                grad_conv[rows, lanes] = (grad_out * query[rows, lanes].astype(f32)).astype(bf16)

        copy = remote(
            grad_conv.at[pl.ds(0, TAPS), columns(chunk)],
            grad_conv.at[pl.ds(row_count, TAPS), columns(chunk)],
            (head_send, head_recv), chunk, {"ctx": previous},
        )
        copy.start()
        head_copies.append(copy)
        send_home(4, stage4, out4, chunk)
        send_home(0, stage0, out0, chunk)

    flip = jnp.where(ramp(0) + ramp(1) == NEAR - 1, 1.0, 0.0)

    @pl.loop(0, tiles)
    def _(tile):
        lanes = lanes_of(tile)
        grads = jnp.concatenate([grad_conv[block_rows(b), lanes] for b in range(blocks)], axis=1)
        flipped = dot(flip.astype(bf16), grads)
        group = lane_group(NEAR, blocks * LANES)
        for g in range(TILE_GROUPS):
            left[block_rows(g)] = jnp.where(group == g, flipped, 0.0).astype(bf16)
        right = jnp.concatenate(
            [medium_input[NEAR * b : NEAR * (b + 2), lanes] for b in range(blocks)], axis=1
        )
        products = lax.dot_general(
            left[...], right, (((1,), (1,)), ((), ())), preferred_element_type=f32
        )
        rows = []
        for g in range(TILE_GROUPS):
            turned = pltpu.roll(products[block_rows(g)], 0, 1, stride=1, stride_axis=0)
            rows.append(jnp.sum(turned[:, NEAR:], axis=0, keepdims=True))
        sums[pl.ds(pl.multiple_of(tile * TILE_GROUPS, TILE_GROUPS), TILE_GROUPS)] = (
            jnp.concatenate(rows, axis=0)
        )

    core_sums[place.core] = sums[...]
    sum_sems = (sum_send, sum_recv)
    sum_copies = gather(core_sums, place.core, [place.partner], sum_sems, 0)

    for chunk in range(CHUNKS):
        head_copies[chunk].wait_recv()

        @pl.when(me == devices - 1)
        def _():
            grad_conv[row_count:, columns(chunk)] = jnp.zeros((TAPS, part), bf16)

        @pl.loop(chunk * tiles // CHUNKS, (chunk + 1) * tiles // CHUNKS)
        def _(tile):
            lanes = lanes_of(tile)
            fill_medium_table(table, adjoint_row, tile)
            for pair in range(blocks // 2):
                both = medium_pair(table, grad_conv, lanes, pair)
                for half in range(2):
                    rows = block_rows(2 * pair + half)
                    grad_input = both[:, LANES * half : LANES * (half + 1)]
                    stage1[rows, lanes] = (grad_input * value[rows, lanes].astype(f32)).astype(bf16)
                    stage2[rows, lanes] = (grad_input * key[rows, lanes].astype(f32)).astype(bf16)

        send_home(1, stage1, out1, chunk)
        send_home(2, stage2, out2, chunk)
        if chunk == 0:
            finish(sum_copies)
            y_sums[place.y] = core_sums[0] + core_sums[1]
            sum_copies = gather(y_sums, place.y, place.y_peers, sum_sems, 1)
        if chunk == 1:
            finish(sum_copies)
            x_sums[place.x] = sum(y_sums[s] for s in range(1, place.size_y)) + y_sums[0]
            sum_copies = gather(x_sums, place.x, place.x_peers, sum_sems, place.size_y)
    finish(sum_copies)
    summed = sum(x_sums[s] for s in range(1, place.size_x)) + x_sums[0]
    filter_out[...] = (
        jnp.dot(summed, flip, precision=highest, preferred_element_type=f32) * scale
    )

    for copy in cot_copies + tail_copies + head_copies:
        copy.wait_send()
    for copy in own_copies:
        copy.wait()
    finish(out_copies)


def store_kernel(*refs):
    sems = refs[-1]
    count = (len(refs) - 1) // 2
    copies = [
        pltpu.make_async_copy(refs[n], refs[count + n], sems.at[n]) for n in range(count)
    ]
    for copy in copies:
        copy.start()
    for copy in copies:
        copy.wait()


def on_device(
    sizes, grad_out, query_medium, key_medium, value_medium, query_modal, key_modal,
    medium_filter, modal_decay, modal_residue,
):
    row_count, channels = query_medium.shape
    blocks = row_count // NEAR
    groups, modes = modal_decay.shape
    devices = lax.axis_size("ctx")
    size_z = lax.axis_size("ch")
    size_x, size_y, _ = sizes
    output = jax.ShapeDtypeStruct(grad_out.shape, bf16)
    filter_output = jax.ShapeDtypeStruct((groups, TAPS), f32)
    scale = 1.0 / math.sqrt(row_count * devices * GS)
    data = pltpu.VMEM((row_count, channels), bf16)
    longer = pltpu.VMEM((row_count + TAPS, channels), bf16)
    states = pltpu.VMEM((blocks, modes, channels), f32)
    state = pltpu.VMEM((modes, channels), f32)

    def joins(width):
        return [pltpu.VMEM((n, modes, width // 2), f32) for n in (2, size_y, size_x, 2)]

    dma = pltpu.SemaphoreType.DMA
    square = (groups, TAPS)
    whole = pl.BlockSpec(memory_space=pl.ANY)
    local = pl.BlockSpec(memory_space=pltpu.VMEM)
    outs = pl.pallas_call(
        lambda *refs: whole_kernel(sizes, scale, *refs),
        in_specs=[whole] * 6 + [local] * 3,
        out_shape=(pltpu.VMEM(grad_out.shape, bf16),) * 5 + (filter_output,),
        out_specs=(local,) * 6,
        scratch_shapes=[data] * 6
        + [longer, pltpu.VMEM((row_count, channels), f32), data, longer]
        + [data] * 5
        + [states] * 2 + [state] * 5
        + joins(channels // 2) * 2 + joins(channels)
        + [pltpu.VMEM((groups * modes // LANES, LANES), f32)] * 2
        + [pltpu.VMEM((groups, 2 * TAPS), f32)] * 2
        + [pltpu.VMEM((TILE_GROUPS * NEAR, 2 * NEAR), bf16),
           pltpu.VMEM((2 * NEAR, blocks * LANES), bf16),
           pltpu.VMEM((TILE_GROUPS * NEAR, blocks * LANES), bf16)]
        + [pltpu.VMEM(square, f32)]
        + [pltpu.VMEM((n,) + square, f32) for n in (2, size_y, size_x)]
        + [dma((5,))] + [dma((size_z - 1, CHUNKS))] * 2 + [dma((CHUNKS,))] * 4
        + [dma((size_x + size_y,))] * 6 + [dma((size_x + size_y,))] * 2
        + [dma((5, size_z - 1, CHUNKS))] * 2 + [dma((6,))],
        compiler_params=pltpu.CompilerParams(
            collective_id=0, has_side_effects=True, vmem_limit_bytes=48 * 1024 * 1024
        ),
    )(
        grad_out, query_medium, key_medium, value_medium, query_modal, key_modal,
        medium_filter, modal_decay.T, modal_residue.T,
    )
    stored = pl.pallas_call(
        store_kernel,
        in_specs=[local] * 5,
        out_shape=(output,) * 5,
        out_specs=(whole,) * 5,
        scratch_shapes=[dma((5,))],
        compiler_params=pltpu.CompilerParams(vmem_limit_bytes=2 * 1024 * 1024),
    )(*[pltpu.with_memory_space_constraint(out, pltpu.VMEM) for out in outs[:5]])
    return tuple(stored) + (outs[5],)


def solution(mesh):
    count = mesh.shape["ctx"] // 2
    side = math.isqrt(count)
    sizes = (side, count // side, 2)

    def body(*args):
        return on_device(sizes, *args)

    rows = P(("ctx", "ch"), None)
    groups = P("ch", None)
    return jax.shard_map(
        body,
        mesh=mesh,
        in_specs=(rows,) + (P("ctx", "ch"),) * 5 + (groups,) * 3,
        out_specs=(rows,) * 5 + (groups,),
        check_vma=False,
    )
```

```python
import math

import jax
import jax.numpy as jnp
from jax import lax
from jax.experimental import pallas as pl
from jax.experimental.pallas import tpu as pltpu
from jax.sharding import PartitionSpec as P

GS = 16
TAPS = 128
NEAR = 128
LANES = 128
TILE_GROUPS = LANES // GS
BOUNDS = (0, 2, 6, 9, 12, 16)
CHUNKS = len(BOUNDS) - 1
MESH = pl.DeviceIdType.MESH

f32 = jnp.float32
bf16 = jnp.bfloat16
highest = lax.Precision.HIGHEST


def dot(a, b):
    return jnp.dot(a, b, preferred_element_type=f32)


def iota(shape, axis):
    return lax.broadcasted_iota(jnp.int32, shape, axis)


def ramp(axis):
    return iota((NEAR, LANES), axis)


def lane_group(rows, columns):
    lane = iota((rows, columns), 1)
    return jnp.bitwise_and(lax.shift_right_logical(lane, 4), TILE_GROUPS - 1)


def pick(stacked, rows, columns):
    group = lane_group(rows, columns)
    kept = stacked[0:rows]
    for g in range(1, TILE_GROUPS):
        kept = jnp.where(group == g, stacked[g * rows : (g + 1) * rows], kept)
    return kept


def skewed(row, height):
    wide = jnp.broadcast_to(row, (height, row.shape[1]))
    return pltpu.roll(wide, 0, 1, stride=1, stride_axis=0)


def split(value):
    high = value.astype(bf16)
    return high, (value - high.astype(f32)).astype(bf16)


def product(a, b):
    return (a.astype(f32) * b.astype(f32)).astype(bf16)


def block_rows(b):
    return slice(NEAR * b, NEAR * (b + 1))


def block_states(weight, data):
    high, low = split(weight.T)
    left = jnp.concatenate([high, low], axis=1)
    right = jnp.concatenate([data, data], axis=0)
    return pick(dot(left, right), weight.shape[1] // TILE_GROUPS, data.shape[1])


def fill_medium_table(table_ref, row_ref, tile):
    rows = row_ref[pl.ds(pl.multiple_of(tile * TILE_GROUPS, TILE_GROUPS), TILE_GROUPS)]
    for g in range(TILE_GROUPS):
        table_ref[block_rows(g)] = skewed(rows[g : g + 1], NEAR).astype(bf16)


def medium_pair(table_ref, data_ref, lanes, pair):
    low = 2 * pair * NEAR
    right = jnp.concatenate(
        [data_ref[low : low + 2 * NEAR, lanes], data_ref[low + NEAR : low + 3 * NEAR, lanes]],
        axis=1,
    )
    return pick(dot(table_ref[...], right), NEAR, 2 * LANES)


def fill_modal_table(table_ref, log_row, residue_row, modes, adjoint):
    row, lane = ramp(0), ramp(1)
    lag = row if adjoint else jnp.bitwise_and(NEAR - row, NEAR - 1)
    terms = residue_row * jnp.exp(log_row * lag.astype(f32))
    member = jnp.where(lane_group(TILE_GROUPS, LANES) == iota((TILE_GROUPS, LANES), 0), 1.0, 0.0)
    taps = lax.dot_general(
        member, terms, (((1,), (1,)), ((), ())), precision=highest, preferred_element_type=f32
    )
    small = iota((TILE_GROUPS, LANES), 1)

    def three(value):
        turned = pltpu.roll(
            jnp.broadcast_to(value, (TILE_GROUPS, LANES)), 0, 1, stride=modes, stride_axis=0
        )
        again, third = pltpu.roll(turned, modes, 1), pltpu.roll(turned, 2 * modes, 1)
        return jnp.where(small < modes, turned, jnp.where(small < 2 * modes, again, third))

    logs, residues = three(log_row), jnp.where(small < 3 * modes, three(residue_row), 0.0)
    near = row <= lane if adjoint else lane <= row
    far_lag = ((NEAR - row) if adjoint else (row + 1)).astype(f32)
    for g in range(TILE_GROUPS):
        q = (TILE_GROUPS - g) % TILE_GROUPS
        table_ref[block_rows(g), 0:LANES] = jnp.where(
            near, skewed(taps[g : g + 1], NEAR), 0.0
        ).astype(bf16)
        far = residues[q : q + 1] * jnp.exp(logs[q : q + 1] * far_lag)
        high = far.astype(bf16).astype(f32)
        table_ref[block_rows(g), LANES:] = jnp.where(
            lane < 2 * modes, high, far - high
        ).astype(bf16)


def modal_blocks(table_ref, data_ref, states):
    high, low = split(states)
    modes = states.shape[0]
    data_ref[NEAR : NEAR + modes] = high
    data_ref[NEAR + modes : NEAR + 2 * modes] = low
    data_ref[NEAR + 2 * modes : NEAR + 3 * modes] = high
    parts = []
    for pair in range(data_ref.shape[1] // (2 * LANES)):
        right = data_ref[:, 2 * LANES * pair : 2 * LANES * (pair + 1)]
        both = pick(dot(table_ref[...], right), NEAR, 2 * LANES)
        parts += [both[:, 0:LANES], both[:, LANES:]]
    return parts


class Place:
    def __init__(self, sizes):
        self.size_x, self.size_y, _ = sizes
        self.me = lax.axis_index("ctx")
        self.core = lax.rem(self.me, 2)
        self.y = lax.rem(lax.div(self.me, 2), self.size_y)
        self.x = lax.div(self.me, 2 * self.size_y)
        self.partner = self.index(self.x, self.y, 1 - self.core)
        self.y_peers = [
            self.index(self.x, lax.rem(self.y + k, self.size_y), self.core)
            for k in range(1, self.size_y)
        ]
        self.x_peers = [
            self.index(lax.rem(self.x + k, self.size_x), self.y, self.core)
            for k in range(1, self.size_x)
        ]

    def index(self, x, y, core):
        return (x * self.size_y + y) * 2 + core


def remote(source, target, sems, slot, peer):
    return pltpu.make_async_remote_copy(
        src_ref=source, dst_ref=target, send_sem=sems[0].at[slot], recv_sem=sems[1].at[slot],
        device_id=peer, device_id_type=MESH,
    )


def gather(buffer, place, peers, sems, base):
    copies = [
        remote(buffer.at[place], buffer.at[place], sems, base + k, {"ctx": peer})
        for k, peer in enumerate(peers)
    ]
    for copy in copies:
        copy.start()
    return copies


def finish(copies):
    for copy in copies:
        copy.wait()


class Join:
    def __init__(
        self, place, forward, low, width, total_ref, result_ref, log_ref, pair, by_y, by_x, out, sems
    ):
        self.place, self.forward = place, forward
        self.total, self.result, self.log = total_ref, result_ref, log_ref
        self.pair, self.by_y, self.by_x, self.out, self.sems = pair, by_y, by_x, out, sems
        half = width // 2
        self.mine = pl.ds(pl.multiple_of(low + place.core * half, LANES), half)
        self.other = pl.ds(pl.multiple_of(low + (1 - place.core) * half, LANES), half)
        self.span = 4 * NEAR

    def decay(self, steps):
        return jnp.exp(self.log[:, self.mine] * (steps * 1.0))

    def start(self):
        place = self.place
        self.copies = [
            remote(self.total.at[:, self.other], self.pair.at[place.core], self.sems, 0,
                   {"ctx": place.partner})
        ]
        self.copies[0].start()
        self.pair[place.core] = self.total[:, self.mine]

    def along_y(self):
        finish(self.copies)
        first, second = (0, 1) if self.forward else (1, 0)
        chip = self.decay(self.span) * self.pair[first] + self.pair[second]
        self.by_y[self.place.y] = chip
        self.copies = gather(self.by_y, self.place.y, self.place.y_peers, self.sems, 1)

    def walk(self, buffer, count, here, decay):
        before = jnp.zeros(buffer.shape[1:], f32)
        whole = before
        for s in range(count) if self.forward else reversed(range(count)):
            value = buffer[s]
            earlier = (s < here) if self.forward else (s > here)
            before = jnp.where(earlier, decay * before + value, before)
            whole = decay * whole + value
        return before, whole

    def along_x(self):
        finish(self.copies)
        place = self.place
        self.before, whole = self.walk(self.by_y, place.size_y, place.y, self.decay(2 * self.span))
        self.out[1] = self.before
        self.by_x[place.x] = whole
        self.copies = gather(self.by_x, place.x, place.x_peers, self.sems, place.size_y)

    def share(self):
        finish(self.copies)
        place = self.place
        chip = self.decay(2 * self.span)
        before, _ = self.walk(
            self.by_x, place.size_x, place.x, self.decay(2 * self.span * place.size_y)
        )
        inner = place.y if self.forward else place.size_y - 1 - place.y
        for k in range(place.size_y - 1):
            before = jnp.where(k < inner, chip * before, before)
        near = self.out[1] + before
        first = 0 if self.forward else 1
        far = self.decay(self.span) * near + self.pair[first]
        is_first = place.core == first
        self.result[:, self.mine] = jnp.where(is_first, near, far)
        self.out[0] = jnp.where(is_first, far, near)
        self.copies = [
            remote(self.out.at[0], self.result.at[:, self.mine], self.sems,
                   place.size_y + place.size_x - 1, {"ctx": place.partner})
        ]
        self.copies[0].start()

    def end(self):
        finish(self.copies)


def whole_kernel(
    sizes, scale,
    cotangent_in, query_in, key_in, value_in, query_modal_in, key_modal_in,
    filter_ref, decay_ref, residue_ref,
    out0, out1, out2, out3, out4, filter_out,
    query, key, value, query_modal, key_modal, cotangent,
    medium_input, conv, medium_out, grad_conv,
    stage0, stage1, stage2, stage3, stage4,
    end_states, start_states, own_total, own_adjoint, entering, arriving, log_rows,
    pair_f, y_f, x_f, o_f, pair_s, y_s, x_s, o_s, pair_b, y_b, x_b, o_b,
    decay_rows, residue_rows, forward_row, adjoint_row, table, wide, left, sums, core_sums, y_sums, x_sums,
    load_sem, cot_send, cot_recv, tail_send, tail_recv, head_send, head_recv,
    join_send, join_recv, join2_send, join2_recv, back_send, back_recv, sum_send, sum_recv,
    out_send, out_recv, own_sem,
):
    place = Place(sizes)
    me, z = place.me, lax.axis_index("ch")
    size_z = lax.axis_size("ch")
    devices = lax.axis_size("ctx")
    row_count, channels = query.shape
    blocks = row_count // NEAR
    tiles = channels // LANES
    modes, groups = decay_ref.shape
    edges = [tiles * bound // BOUNDS[-1] for bound in BOUNDS]
    following = lax.rem(me + 1, devices)
    previous = lax.rem(me + devices - 1, devices)

    def width(chunk):
        return (edges[chunk + 1] - edges[chunk]) * LANES

    def columns(chunk):
        return pl.ds(edges[chunk] * LANES, width(chunk))

    def columns_of(owner, chunk):
        start = owner * channels + edges[chunk] * LANES
        return pl.ds(pl.multiple_of(start, LANES), width(chunk))

    loads = [
        pltpu.make_async_copy(source, target, load_sem.at[n])
        for n, (source, target) in enumerate(
            [(key_in, key), (value_in, value), (query_in, query), (key_modal_in, key_modal),
             (query_modal_in, query_modal)]
        )
    ]
    for copy in loads:
        copy.start()

    z_peers = [lax.rem(z + k, size_z) for k in range(1, size_z)]
    barrier = pltpu.get_barrier_semaphore()
    for peer in z_peers:
        pl.semaphore_signal(barrier, inc=1, device_id={"ch": peer}, device_id_type=MESH)
    ring = [place.partner] + place.y_peers + place.x_peers + [following, previous]
    for peer in ring:
        pl.semaphore_signal(barrier, inc=1, device_id={"ctx": peer}, device_id_type=MESH)
    pl.semaphore_wait(barrier, len(z_peers) + len(ring))

    own_rows = pl.ds(pl.multiple_of(z * NEAR, NEAR), NEAR)
    own_columns = pl.ds(pl.multiple_of(z * channels, channels), channels)

    cot_copies = []
    for chunk in range(CHUNKS):
        for k, peer in enumerate(z_peers):
            source = columns_of(peer, chunk)
            copy = remote(
                cotangent_in.at[:, source], cotangent.at[own_rows, columns(chunk)],
                (cot_send.at[k], cot_recv.at[k]), chunk, {"ch": peer},
            )
            copy.start()
            cot_copies.append(copy)
    cot_own = pltpu.make_async_copy(
        cotangent_in.at[:, own_columns], cotangent.at[own_rows], own_sem.at[5]
    )
    cot_own.start()

    loads[0].wait()
    loads[1].wait()
    last = slice(row_count - TAPS, row_count)
    medium_input[row_count:] = product(key[last], value[last])
    tail_copies = [
        remote(
            medium_input.at[pl.ds(row_count, TAPS), columns(c)],
            medium_input.at[pl.ds(0, TAPS), columns(c)],
            (tail_send, tail_recv), c, {"ctx": following},
        )
        for c in range(CHUNKS)
    ]
    for copy in tail_copies:
        copy.start()

    taps_in = filter_ref[...]
    turn = jnp.where(
        iota((TAPS, 2 * TAPS), 0) + iota((TAPS, 2 * TAPS), 1) == TAPS, 1.0, 0.0
    ).astype(bf16)
    forward_row[...] = dot(taps_in, turn)
    adjoint_row[:, 0:TAPS] = taps_in.astype(f32)
    adjoint_row[:, TAPS:] = jnp.zeros(taps_in.shape, f32)
    wide[NEAR + 3 * modes :] = jnp.zeros((NEAR - 3 * modes, wide.shape[1]), bf16)
    own_mode = jnp.bitwise_and(iota((modes, LANES), 1), modes - 1) == iota((modes, LANES), 0)

    def lanes_of(tile):
        return pl.ds(pl.multiple_of(tile * LANES, LANES), LANES)

    @pl.loop(0, tiles)
    def _(tile):
        spread = jnp.where(
            iota((groups, LANES), 0)
            == tile * TILE_GROUPS + lax.shift_right_logical(iota((groups, LANES), 1), 4),
            1.0, 0.0,
        )

        def per_channel(ref):
            return jnp.dot(ref[...], spread, precision=highest, preferred_element_type=f32)

        def per_mode(value):
            return jnp.sum(jnp.where(own_mode, value, 0.0), axis=0, keepdims=True)

        decay = per_channel(decay_ref)
        log_rows[:, lanes_of(tile)] = jnp.log(decay)
        decay_rows[pl.ds(tile, 1)] = per_mode(decay)
        residue_rows[pl.ds(tile, 1)] = per_mode(per_channel(residue_ref))

    loads[2].wait()
    loads[3].wait()
    early = slice(0, row_count - TAPS)

    def medium_forward(chunk):
        tail_copies[chunk].wait_recv()

        @pl.when(me == 0)
        def _():
            medium_input[0:TAPS, columns(chunk)] = jnp.zeros((TAPS, width(chunk)), bf16)

        @pl.loop(edges[chunk], edges[chunk + 1])
        def _(tile):
            lanes = lanes_of(tile)
            medium_input[TAPS:row_count, lanes] = product(key[early, lanes], value[early, lanes])
            fill_medium_table(table, forward_row, tile)
            inputs = []
            for pair in range(blocks // 2):
                both = medium_pair(table, medium_input, lanes, pair)
                for half in range(2):
                    rows = block_rows(2 * pair + half)
                    part_conv = both[:, LANES * half : LANES * (half + 1)]
                    conv[rows, lanes] = part_conv
                    out = (query[rows, lanes].astype(f32) * part_conv).astype(bf16)
                    medium_out[rows, lanes] = out
                    inputs.append(product(key_modal[rows, lanes], out))
            log_row = jnp.log(decay_rows[pl.ds(tile, 1)])
            weight = jnp.exp(log_row * (NEAR - 1 - ramp(0)).astype(f32))
            states = block_states(weight, jnp.concatenate(inputs, axis=1))
            step = jnp.exp(log_rows[:, lanes] * NEAR)
            total = jnp.zeros((modes, LANES), f32)
            for b in range(blocks):
                state = states[:, LANES * b : LANES * (b + 1)]
                end_states[b, :, lanes] = state
                total = step * total + state
            own_total[:, lanes] = total

    def adjoint_states(chunk):
        for copy in cot_copies[(size_z - 1) * chunk : (size_z - 1) * (chunk + 1)]:
            copy.wait_recv()

        @pl.loop(edges[chunk], edges[chunk + 1])
        def _(tile):
            lanes = lanes_of(tile)
            grads = jnp.concatenate(
                [product(cotangent[block_rows(b), lanes], query_modal[block_rows(b), lanes])
                 for b in range(blocks)],
                axis=1,
            )
            log_row = jnp.log(decay_rows[pl.ds(tile, 1)])
            states = block_states(jnp.exp(log_row * ramp(0).astype(f32)), grads)
            step = jnp.exp(log_rows[:, lanes] * NEAR)
            total = jnp.zeros((modes, LANES), f32)
            for b in reversed(range(blocks)):
                state = states[:, LANES * b : LANES * (b + 1)]
                start_states[b, :, lanes] = state
                total = step * total + state
            own_adjoint[:, lanes] = total

    out_copies, own_copies = [], []

    def send_home(n, stage, out, chunk):
        for k, peer in enumerate(z_peers):
            rows = pl.ds(pl.multiple_of(peer * NEAR, NEAR), NEAR)
            target = columns_of(z, chunk)
            copy = remote(
                stage.at[rows, columns(chunk)], out.at[:, target],
                (out_send.at[n, k], out_recv.at[n, k]), chunk, {"ch": peer},
            )
            copy.start()
            out_copies.append(copy)
        if chunk == CHUNKS - 1:
            copy = pltpu.make_async_copy(
                stage.at[own_rows], out.at[:, own_columns], own_sem.at[n]
            )
            copy.start()
            own_copies.append(copy)

    def modal_forward(chunk):
        @pl.loop(edges[chunk], edges[chunk + 1])
        def _(tile):
            lanes = lanes_of(tile)
            log_row = jnp.log(decay_rows[pl.ds(tile, 1)])
            fill_modal_table(table, log_row, residue_rows[pl.ds(tile, 1)], modes, False)
            step = jnp.exp(log_rows[:, lanes] * NEAR)
            carried = entering[:, lanes]
            befores = []
            for b in range(blocks):
                wide[0:NEAR, LANES * b : LANES * (b + 1)] = product(
                    key_modal[block_rows(b), lanes], medium_out[block_rows(b), lanes]
                )
                befores.append(carried)
                carried = step * carried + end_states[b, :, lanes]
            parts = modal_blocks(table, wide, jnp.concatenate(befores, axis=1))
            for b in range(blocks):
                rows = block_rows(b)
                stage3[rows, lanes] = (cotangent[rows, lanes].astype(f32) * parts[b]).astype(bf16)

        send_home(3, stage3, out3, chunk)

    early_width = edges[2] * LANES
    first = Join(place, True, 0, early_width, own_total, entering, log_rows,
                 pair_f, y_f, x_f, o_f, (join_send, join_recv))
    second = Join(place, True, early_width, channels - early_width, own_total, entering, log_rows,
                  pair_s, y_s, x_s, o_s, (join2_send, join2_recv))
    backward = Join(place, False, 0, channels, own_adjoint, arriving, log_rows,
                    pair_b, y_b, x_b, o_b, (back_send, back_recv))
    medium_forward(0)
    medium_forward(1)
    first.start()
    medium_forward(2)
    first.along_y()
    medium_forward(3)
    first.along_x()
    medium_forward(4)
    second.start()
    first.share()
    cot_own.wait()
    loads[4].wait()
    adjoint_states(0)
    second.along_y()
    adjoint_states(1)
    first.end()
    modal_forward(0)
    second.along_x()
    modal_forward(1)
    second.share()
    adjoint_states(2)
    adjoint_states(3)
    adjoint_states(4)
    backward.start()
    second.end()
    modal_forward(2)
    backward.along_y()
    modal_forward(3)
    backward.along_x()
    modal_forward(4)
    backward.share()
    backward.end()

    head_copies = []
    for chunk in range(CHUNKS):

        @pl.loop(edges[chunk], edges[chunk + 1])
        def _(tile):
            lanes = lanes_of(tile)
            log_row = jnp.log(decay_rows[pl.ds(tile, 1)])
            fill_modal_table(table, log_row, residue_rows[pl.ds(tile, 1)], modes, True)
            step = jnp.exp(log_rows[:, lanes] * NEAR)
            carried = arriving[:, lanes]
            nexts = [carried] * blocks
            for b in reversed(range(blocks)):
                wide[0:NEAR, LANES * b : LANES * (b + 1)] = product(
                    cotangent[block_rows(b), lanes], query_modal[block_rows(b), lanes]
                )
                nexts[b] = carried
                carried = step * carried + start_states[b, :, lanes]
            parts = modal_blocks(table, wide, jnp.concatenate(nexts, axis=1))
            for b in range(blocks):
                rows = block_rows(b)
                stage4[rows, lanes] = (parts[b] * medium_out[rows, lanes].astype(f32)).astype(bf16)
                grad_out = parts[b] * key_modal[rows, lanes].astype(f32)
                stage0[rows, lanes] = (grad_out * conv[rows, lanes]).astype(bf16)
                grad_conv[rows, lanes] = (grad_out * query[rows, lanes].astype(f32)).astype(bf16)

        copy = remote(
            grad_conv.at[pl.ds(0, TAPS), columns(chunk)],
            grad_conv.at[pl.ds(row_count, TAPS), columns(chunk)],
            (head_send, head_recv), chunk, {"ctx": previous},
        )
        copy.start()
        head_copies.append(copy)
        send_home(4, stage4, out4, chunk)
        send_home(0, stage0, out0, chunk)

    flip = jnp.where(ramp(0) + ramp(1) == NEAR - 1, 1.0, 0.0)

    @pl.loop(0, tiles)
    def _(tile):
        lanes = lanes_of(tile)
        grads = jnp.concatenate([grad_conv[block_rows(b), lanes] for b in range(blocks)], axis=1)
        flipped = dot(flip.astype(bf16), grads)
        group = lane_group(NEAR, blocks * LANES)
        for g in range(TILE_GROUPS):
            left[block_rows(g)] = jnp.where(group == g, flipped, 0.0).astype(bf16)
        right = jnp.concatenate(
            [medium_input[NEAR * b : NEAR * (b + 2), lanes] for b in range(blocks)], axis=1
        )
        products = lax.dot_general(
            left[...], right, (((1,), (1,)), ((), ())), preferred_element_type=f32
        )
        rows = []
        for g in range(TILE_GROUPS):
            turned = pltpu.roll(products[block_rows(g)], 0, 1, stride=1, stride_axis=0)
            rows.append(jnp.sum(turned[:, NEAR:], axis=0, keepdims=True))
        sums[pl.ds(pl.multiple_of(tile * TILE_GROUPS, TILE_GROUPS), TILE_GROUPS)] = (
            jnp.concatenate(rows, axis=0)
        )

    core_sums[place.core] = sums[...]
    sum_sems = (sum_send, sum_recv)
    sum_copies = gather(core_sums, place.core, [place.partner], sum_sems, 0)

    for chunk in range(CHUNKS):
        head_copies[chunk].wait_recv()

        @pl.when(me == devices - 1)
        def _():
            grad_conv[row_count:, columns(chunk)] = jnp.zeros((TAPS, width(chunk)), bf16)

        @pl.loop(edges[chunk], edges[chunk + 1])
        def _(tile):
            lanes = lanes_of(tile)
            fill_medium_table(table, adjoint_row, tile)
            for pair in range(blocks // 2):
                both = medium_pair(table, grad_conv, lanes, pair)
                for half in range(2):
                    rows = block_rows(2 * pair + half)
                    grad_input = both[:, LANES * half : LANES * (half + 1)]
                    stage1[rows, lanes] = (grad_input * value[rows, lanes].astype(f32)).astype(bf16)
                    stage2[rows, lanes] = (grad_input * key[rows, lanes].astype(f32)).astype(bf16)

        send_home(1, stage1, out1, chunk)
        send_home(2, stage2, out2, chunk)
        if chunk == 0:
            finish(sum_copies)
            y_sums[place.y] = core_sums[0] + core_sums[1]
            sum_copies = gather(y_sums, place.y, place.y_peers, sum_sems, 1)
        if chunk == 1:
            finish(sum_copies)
            x_sums[place.x] = sum(y_sums[s] for s in range(1, place.size_y)) + y_sums[0]
            sum_copies = gather(x_sums, place.x, place.x_peers, sum_sems, place.size_y)
    finish(sum_copies)
    summed = sum(x_sums[s] for s in range(1, place.size_x)) + x_sums[0]
    filter_out[...] = (
        jnp.dot(summed, flip, precision=highest, preferred_element_type=f32) * scale
    )

    for copy in cot_copies + tail_copies + head_copies:
        copy.wait_send()
    for copy in own_copies:
        copy.wait()
    finish(out_copies)


def store_kernel(*refs):
    sems = refs[-1]
    count = (len(refs) - 1) // 2
    copies = [
        pltpu.make_async_copy(refs[n], refs[count + n], sems.at[n]) for n in range(count)
    ]
    for copy in copies:
        copy.start()
    for copy in copies:
        copy.wait()


def on_device(
    sizes, grad_out, query_medium, key_medium, value_medium, query_modal, key_modal,
    medium_filter, modal_decay, modal_residue,
):
    row_count, channels = query_medium.shape
    blocks = row_count // NEAR
    groups, modes = modal_decay.shape
    devices = lax.axis_size("ctx")
    size_z = lax.axis_size("ch")
    size_x, size_y, _ = sizes
    output = jax.ShapeDtypeStruct(grad_out.shape, bf16)
    filter_output = jax.ShapeDtypeStruct((groups, TAPS), f32)
    scale = 1.0 / math.sqrt(row_count * devices * GS)
    data = pltpu.VMEM((row_count, channels), bf16)
    longer = pltpu.VMEM((row_count + TAPS, channels), bf16)
    states = pltpu.VMEM((blocks, modes, channels), f32)
    state = pltpu.VMEM((modes, channels), f32)

    early_width = channels * BOUNDS[2] // BOUNDS[-1]

    def joins(width):
        return [pltpu.VMEM((n, modes, width // 2), f32) for n in (2, size_y, size_x, 2)]

    dma = pltpu.SemaphoreType.DMA
    square = (groups, TAPS)
    whole = pl.BlockSpec(memory_space=pl.ANY)
    local = pl.BlockSpec(memory_space=pltpu.VMEM)
    outs = pl.pallas_call(
        lambda *refs: whole_kernel(sizes, scale, *refs),
        in_specs=[whole] * 6 + [local] * 3,
        out_shape=(pltpu.VMEM(grad_out.shape, bf16),) * 5 + (filter_output,),
        out_specs=(local,) * 6,
        scratch_shapes=[data] * 6
        + [longer, pltpu.VMEM((row_count, channels), f32), data, longer]
        + [data] * 5
        + [states] * 2 + [state] * 5
        + joins(early_width) + joins(channels - early_width) + joins(channels)
        + [pltpu.VMEM((groups * modes // LANES, LANES), f32)] * 2
        + [pltpu.VMEM((groups, 2 * TAPS), f32)] * 2
        + [pltpu.VMEM((TILE_GROUPS * NEAR, 2 * NEAR), bf16),
           pltpu.VMEM((2 * NEAR, blocks * LANES), bf16),
           pltpu.VMEM((TILE_GROUPS * NEAR, blocks * LANES), bf16)]
        + [pltpu.VMEM(square, f32)]
        + [pltpu.VMEM((n,) + square, f32) for n in (2, size_y, size_x)]
        + [dma((5,))] + [dma((size_z - 1, CHUNKS))] * 2 + [dma((CHUNKS,))] * 4
        + [dma((size_x + size_y,))] * 6 + [dma((size_x + size_y,))] * 2
        + [dma((5, size_z - 1, CHUNKS))] * 2 + [dma((6,))],
        compiler_params=pltpu.CompilerParams(
            collective_id=0, has_side_effects=True, vmem_limit_bytes=48 * 1024 * 1024
        ),
    )(
        grad_out, query_medium, key_medium, value_medium, query_modal, key_modal,
        medium_filter, modal_decay.T, modal_residue.T,
    )
    stored = pl.pallas_call(
        store_kernel,
        in_specs=[local] * 5,
        out_shape=(output,) * 5,
        out_specs=(whole,) * 5,
        scratch_shapes=[dma((5,))],
        compiler_params=pltpu.CompilerParams(vmem_limit_bytes=2 * 1024 * 1024),
    )(*[pltpu.with_memory_space_constraint(out, pltpu.VMEM) for out in outs[:5]])
    return tuple(stored) + (outs[5],)


def solution(mesh):
    count = mesh.shape["ctx"] // 2
    side = math.isqrt(count)
    sizes = (side, count // side, 2)

    def body(*args):
        return on_device(sizes, *args)

    rows = P(("ctx", "ch"), None)
    groups = P("ch", None)
    return jax.shard_map(
        body,
        mesh=mesh,
        in_specs=(rows,) + (P("ctx", "ch"),) * 5 + (groups,) * 3,
        out_specs=(rows,) * 5 + (groups,),
        check_vma=False,
    )
```

```python
import math

import jax
import jax.numpy as jnp
from jax import lax
from jax.experimental import pallas as pl
from jax.experimental.pallas import tpu as pltpu
from jax.sharding import PartitionSpec as P

GS = 16
TAPS = 128
NEAR = 128
LANES = 128
TILE_GROUPS = LANES // GS
BOUNDS = (0, 2, 6, 9, 12, 16)
CHUNKS = len(BOUNDS) - 1
MESH = pl.DeviceIdType.MESH

f32 = jnp.float32
bf16 = jnp.bfloat16
highest = lax.Precision.HIGHEST


def dot(a, b):
    return jnp.dot(a, b, preferred_element_type=f32)


def iota(shape, axis):
    return lax.broadcasted_iota(jnp.int32, shape, axis)


def ramp(axis):
    return iota((NEAR, LANES), axis)


def lane_group(rows, columns):
    lane = iota((rows, columns), 1)
    return jnp.bitwise_and(lax.shift_right_logical(lane, 4), TILE_GROUPS - 1)


def pick(stacked, rows, columns):
    group = lane_group(rows, columns)
    kept = stacked[0:rows]
    for g in range(1, TILE_GROUPS):
        kept = jnp.where(group == g, stacked[g * rows : (g + 1) * rows], kept)
    return kept


def skewed(row, height):
    wide = jnp.broadcast_to(row, (height, row.shape[1]))
    return pltpu.roll(wide, 0, 1, stride=1, stride_axis=0)


def split(value):
    high = value.astype(bf16)
    return high, (value - high.astype(f32)).astype(bf16)


def product(a, b):
    return (a.astype(f32) * b.astype(f32)).astype(bf16)


def block_rows(b):
    return slice(NEAR * b, NEAR * (b + 1))


def block_states(weight, data):
    high, low = split(weight.T)
    left = jnp.concatenate([high, low], axis=1)
    right = jnp.concatenate([data, data], axis=0)
    return pick(dot(left, right), weight.shape[1] // TILE_GROUPS, data.shape[1])


def fill_medium_table(table_ref, row_ref, tile):
    rows = row_ref[pl.ds(pl.multiple_of(tile * TILE_GROUPS, TILE_GROUPS), TILE_GROUPS)]
    for g in range(TILE_GROUPS):
        table_ref[block_rows(g)] = skewed(rows[g : g + 1], NEAR).astype(bf16)


def medium_pair(table_ref, data_ref, lanes, pair):
    low = 2 * pair * NEAR
    right = jnp.concatenate(
        [data_ref[low : low + 2 * NEAR, lanes], data_ref[low + NEAR : low + 3 * NEAR, lanes]],
        axis=1,
    )
    return pick(dot(table_ref[...], right), NEAR, 2 * LANES)


def fill_modal_table(table_ref, log_row, residue_row, modes, adjoint):
    row, lane = ramp(0), ramp(1)
    lag = row if adjoint else jnp.bitwise_and(NEAR - row, NEAR - 1)
    terms = residue_row * jnp.exp(log_row * lag.astype(f32))
    member = jnp.where(lane_group(TILE_GROUPS, LANES) == iota((TILE_GROUPS, LANES), 0), 1.0, 0.0)
    taps = lax.dot_general(
        member, terms, (((1,), (1,)), ((), ())), precision=highest, preferred_element_type=f32
    )
    small = iota((TILE_GROUPS, LANES), 1)

    def three(value):
        turned = pltpu.roll(
            jnp.broadcast_to(value, (TILE_GROUPS, LANES)), 0, 1, stride=modes, stride_axis=0
        )
        again, third = pltpu.roll(turned, modes, 1), pltpu.roll(turned, 2 * modes, 1)
        return jnp.where(small < modes, turned, jnp.where(small < 2 * modes, again, third))

    logs, residues = three(log_row), jnp.where(small < 3 * modes, three(residue_row), 0.0)
    near = row <= lane if adjoint else lane <= row
    far_lag = ((NEAR - row) if adjoint else (row + 1)).astype(f32)
    for g in range(TILE_GROUPS):
        q = (TILE_GROUPS - g) % TILE_GROUPS
        table_ref[block_rows(g), 0:LANES] = jnp.where(
            near, skewed(taps[g : g + 1], NEAR), 0.0
        ).astype(bf16)
        far = residues[q : q + 1] * jnp.exp(logs[q : q + 1] * far_lag)
        high = far.astype(bf16).astype(f32)
        table_ref[block_rows(g), LANES:] = jnp.where(
            lane < 2 * modes, high, far - high
        ).astype(bf16)


def modal_blocks(table_ref, data_ref, states):
    high, low = split(states)
    modes = states.shape[0]
    data_ref[NEAR : NEAR + modes] = high
    data_ref[NEAR + modes : NEAR + 2 * modes] = low
    data_ref[NEAR + 2 * modes : NEAR + 3 * modes] = high
    parts = []
    for pair in range(data_ref.shape[1] // (2 * LANES)):
        right = data_ref[:, 2 * LANES * pair : 2 * LANES * (pair + 1)]
        both = pick(dot(table_ref[...], right), NEAR, 2 * LANES)
        parts += [both[:, 0:LANES], both[:, LANES:]]
    return parts


class Place:
    def __init__(self, sizes):
        self.size_x, self.size_y, _ = sizes
        self.me = lax.axis_index("ctx")
        self.core = lax.rem(self.me, 2)
        self.y = lax.rem(lax.div(self.me, 2), self.size_y)
        self.x = lax.div(self.me, 2 * self.size_y)
        self.partner = self.index(self.x, self.y, 1 - self.core)
        self.y_peers = [
            self.index(self.x, lax.rem(self.y + k, self.size_y), self.core)
            for k in range(1, self.size_y)
        ]
        self.x_peers = [
            self.index(lax.rem(self.x + k, self.size_x), self.y, self.core)
            for k in range(1, self.size_x)
        ]

    def index(self, x, y, core):
        return (x * self.size_y + y) * 2 + core


def remote(source, target, sems, slot, peer):
    return pltpu.make_async_remote_copy(
        src_ref=source, dst_ref=target, send_sem=sems[0].at[slot], recv_sem=sems[1].at[slot],
        device_id=peer, device_id_type=MESH,
    )


def gather(buffer, place, peers, sems, base):
    copies = [
        remote(buffer.at[place], buffer.at[place], sems, base + k, {"ctx": peer})
        for k, peer in enumerate(peers)
    ]
    for copy in copies:
        copy.start()
    return copies


def finish(copies):
    for copy in copies:
        copy.wait()


class Join:
    def __init__(
        self, place, forward, low, width, total_ref, result_ref, log_ref, pair, by_y, by_x, out, sems
    ):
        self.place, self.forward = place, forward
        self.total, self.result, self.log = total_ref, result_ref, log_ref
        self.pair, self.by_y, self.by_x, self.out, self.sems = pair, by_y, by_x, out, sems
        half = width // 2
        self.mine = pl.ds(pl.multiple_of(low + place.core * half, LANES), half)
        self.other = pl.ds(pl.multiple_of(low + (1 - place.core) * half, LANES), half)
        self.span = 4 * NEAR

    def decay(self, steps):
        return jnp.exp(self.log[:, self.mine] * (steps * 1.0))

    def start(self):
        place = self.place
        self.copies = [
            remote(self.total.at[:, self.other], self.pair.at[place.core], self.sems, 0,
                   {"ctx": place.partner})
        ]
        self.copies[0].start()
        self.pair[place.core] = self.total[:, self.mine]

    def along_y(self):
        finish(self.copies)
        first, second = (0, 1) if self.forward else (1, 0)
        chip = self.decay(self.span) * self.pair[first] + self.pair[second]
        self.by_y[self.place.y] = chip
        self.copies = gather(self.by_y, self.place.y, self.place.y_peers, self.sems, 1)

    def walk(self, buffer, count, here, decay):
        before = jnp.zeros(buffer.shape[1:], f32)
        whole = before
        for s in range(count) if self.forward else reversed(range(count)):
            value = buffer[s]
            earlier = (s < here) if self.forward else (s > here)
            before = jnp.where(earlier, decay * before + value, before)
            whole = decay * whole + value
        return before, whole

    def along_x(self):
        finish(self.copies)
        place = self.place
        self.before, whole = self.walk(self.by_y, place.size_y, place.y, self.decay(2 * self.span))
        self.out[1] = self.before
        self.by_x[place.x] = whole
        self.copies = gather(self.by_x, place.x, place.x_peers, self.sems, place.size_y)

    def share(self):
        finish(self.copies)
        place = self.place
        chip = self.decay(2 * self.span)
        before, _ = self.walk(
            self.by_x, place.size_x, place.x, self.decay(2 * self.span * place.size_y)
        )
        inner = place.y if self.forward else place.size_y - 1 - place.y
        for k in range(place.size_y - 1):
            before = jnp.where(k < inner, chip * before, before)
        near = self.out[1] + before
        first = 0 if self.forward else 1
        far = self.decay(self.span) * near + self.pair[first]
        is_first = place.core == first
        self.result[:, self.mine] = jnp.where(is_first, near, far)
        self.out[0] = jnp.where(is_first, far, near)
        self.copies = [
            remote(self.out.at[0], self.result.at[:, self.mine], self.sems,
                   place.size_y + place.size_x - 1, {"ctx": place.partner})
        ]
        self.copies[0].start()

    def end(self):
        finish(self.copies)


def whole_kernel(
    sizes, scale,
    cotangent_in, query_in, key_in, value_in, query_modal_in, key_modal_in,
    filter_ref, decay_ref, residue_ref,
    out0, out1, out2, out3, out4, filter_out,
    query, key, value, query_modal, key_modal, cotangent,
    medium_input, conv, medium_out, grad_conv,
    stage0, stage1, stage2, stage3, stage4,
    end_states, start_states, own_total, own_adjoint, entering, arriving, log_rows,
    pair_f, y_f, x_f, o_f, pair_s, y_s, x_s, o_s, pair_b, y_b, x_b, o_b,
    decay_rows, residue_rows, forward_row, adjoint_row, table, wide, left, sums, core_sums, y_sums, x_sums,
    load_sem, cot_send, cot_recv, tail_send, tail_recv, head_send, head_recv,
    join_send, join_recv, join2_send, join2_recv, back_send, back_recv, sum_send, sum_recv,
    out_send, out_recv, own_sem,
):
    place = Place(sizes)
    me, z = place.me, lax.axis_index("ch")
    size_z = lax.axis_size("ch")
    devices = lax.axis_size("ctx")
    row_count, channels = query.shape
    blocks = row_count // NEAR
    tiles = channels // LANES
    modes, groups = decay_ref.shape
    edges = [tiles * bound // BOUNDS[-1] for bound in BOUNDS]
    following = lax.rem(me + 1, devices)
    previous = lax.rem(me + devices - 1, devices)

    def width(chunk):
        return (edges[chunk + 1] - edges[chunk]) * LANES

    def columns(chunk):
        return pl.ds(edges[chunk] * LANES, width(chunk))

    def columns_of(owner, chunk):
        start = owner * channels + edges[chunk] * LANES
        return pl.ds(pl.multiple_of(start, LANES), width(chunk))

    loads = [
        pltpu.make_async_copy(source, target, load_sem.at[n])
        for n, (source, target) in enumerate(
            [(key_in, key), (value_in, value), (query_in, query), (key_modal_in, key_modal),
             (query_modal_in, query_modal)]
        )
    ]
    for copy in loads:
        copy.start()

    z_peers = [lax.rem(z + k, size_z) for k in range(1, size_z)]
    barrier = pltpu.get_barrier_semaphore()
    for peer in z_peers:
        pl.semaphore_signal(barrier, inc=1, device_id={"ch": peer}, device_id_type=MESH)
    ring = [place.partner] + place.y_peers + place.x_peers + [following, previous]
    for peer in ring:
        pl.semaphore_signal(barrier, inc=1, device_id={"ctx": peer}, device_id_type=MESH)
    pl.semaphore_wait(barrier, len(z_peers) + len(ring))

    own_rows = pl.ds(pl.multiple_of(z * NEAR, NEAR), NEAR)
    own_columns = pl.ds(pl.multiple_of(z * channels, channels), channels)

    cot_copies = []
    for chunk in range(CHUNKS):
        for k, peer in enumerate(z_peers):
            source = columns_of(peer, chunk)
            copy = remote(
                cotangent_in.at[:, source], cotangent.at[own_rows, columns(chunk)],
                (cot_send.at[k], cot_recv.at[k]), chunk, {"ch": peer},
            )
            copy.start()
            cot_copies.append(copy)
    cot_own = pltpu.make_async_copy(
        cotangent_in.at[:, own_columns], cotangent.at[own_rows], own_sem.at[5]
    )
    cot_own.start()

    loads[0].wait()
    loads[1].wait()
    last = slice(row_count - TAPS, row_count)
    medium_input[row_count:] = product(key[last], value[last])
    tail_copies = [
        remote(
            medium_input.at[pl.ds(row_count, TAPS), columns(c)],
            medium_input.at[pl.ds(0, TAPS), columns(c)],
            (tail_send, tail_recv), c, {"ctx": following},
        )
        for c in range(CHUNKS)
    ]
    for copy in tail_copies:
        copy.start()

    taps_in = filter_ref[...]
    turn = jnp.where(
        iota((TAPS, 2 * TAPS), 0) + iota((TAPS, 2 * TAPS), 1) == TAPS, 1.0, 0.0
    ).astype(bf16)
    forward_row[...] = dot(taps_in, turn)
    adjoint_row[:, 0:TAPS] = taps_in.astype(f32)
    adjoint_row[:, TAPS:] = jnp.zeros(taps_in.shape, f32)
    wide[NEAR + 3 * modes :] = jnp.zeros((NEAR - 3 * modes, wide.shape[1]), bf16)
    own_mode = jnp.bitwise_and(iota((modes, LANES), 1), modes - 1) == iota((modes, LANES), 0)

    def lanes_of(tile):
        return pl.ds(pl.multiple_of(tile * LANES, LANES), LANES)

    @pl.loop(0, tiles)
    def _(tile):
        spread = jnp.where(
            iota((groups, LANES), 0)
            == tile * TILE_GROUPS + lax.shift_right_logical(iota((groups, LANES), 1), 4),
            1.0, 0.0,
        )

        def per_channel(ref):
            return jnp.dot(ref[...], spread, precision=highest, preferred_element_type=f32)

        def per_mode(value):
            return jnp.sum(jnp.where(own_mode, value, 0.0), axis=0, keepdims=True)

        decay = per_channel(decay_ref)
        log_rows[:, lanes_of(tile)] = jnp.log(decay)
        decay_rows[pl.ds(tile, 1)] = per_mode(decay)
        residue_rows[pl.ds(tile, 1)] = per_mode(per_channel(residue_ref))

    loads[2].wait()
    loads[3].wait()
    early = slice(0, row_count - TAPS)

    def medium_forward(chunk):
        tail_copies[chunk].wait_recv()

        @pl.when(me == 0)
        def _():
            medium_input[0:TAPS, columns(chunk)] = jnp.zeros((TAPS, width(chunk)), bf16)

        @pl.loop(edges[chunk], edges[chunk + 1])
        def _(tile):
            lanes = lanes_of(tile)
            medium_input[TAPS:row_count, lanes] = product(key[early, lanes], value[early, lanes])
            fill_medium_table(table, forward_row, tile)
            inputs = []
            for pair in range(blocks // 2):
                both = medium_pair(table, medium_input, lanes, pair)
                for half in range(2):
                    rows = block_rows(2 * pair + half)
                    part_conv = both[:, LANES * half : LANES * (half + 1)]
                    conv[rows, lanes] = part_conv
                    out = (query[rows, lanes].astype(f32) * part_conv).astype(bf16)
                    medium_out[rows, lanes] = out
                    inputs.append(product(key_modal[rows, lanes], out))
            log_row = jnp.log(decay_rows[pl.ds(tile, 1)])
            weight = jnp.exp(log_row * (NEAR - 1 - ramp(0)).astype(f32))
            states = block_states(weight, jnp.concatenate(inputs, axis=1))
            step = jnp.exp(log_rows[:, lanes] * NEAR)
            total = jnp.zeros((modes, LANES), f32)
            for b in range(blocks):
                state = states[:, LANES * b : LANES * (b + 1)]
                end_states[b, :, lanes] = state
                total = step * total + state
            own_total[:, lanes] = total

    def adjoint_states(chunk):
        for copy in cot_copies[(size_z - 1) * chunk : (size_z - 1) * (chunk + 1)]:
            copy.wait_recv()

        @pl.loop(edges[chunk], edges[chunk + 1])
        def _(tile):
            lanes = lanes_of(tile)
            grads = jnp.concatenate(
                [product(cotangent[block_rows(b), lanes], query_modal[block_rows(b), lanes])
                 for b in range(blocks)],
                axis=1,
            )
            log_row = jnp.log(decay_rows[pl.ds(tile, 1)])
            states = block_states(jnp.exp(log_row * ramp(0).astype(f32)), grads)
            step = jnp.exp(log_rows[:, lanes] * NEAR)
            total = jnp.zeros((modes, LANES), f32)
            for b in reversed(range(blocks)):
                state = states[:, LANES * b : LANES * (b + 1)]
                start_states[b, :, lanes] = state
                total = step * total + state
            own_adjoint[:, lanes] = total

    out_copies, own_copies = [], []

    def send_home(n, stage, out, chunk):
        for k, peer in enumerate(z_peers):
            rows = pl.ds(pl.multiple_of(peer * NEAR, NEAR), NEAR)
            target = columns_of(z, chunk)
            copy = remote(
                stage.at[rows, columns(chunk)], out.at[:, target],
                (out_send.at[n, k], out_recv.at[n, k]), chunk, {"ch": peer},
            )
            copy.start()
            out_copies.append(copy)
        if chunk == CHUNKS - 1:
            copy = pltpu.make_async_copy(
                stage.at[own_rows], out.at[:, own_columns], own_sem.at[n]
            )
            copy.start()
            own_copies.append(copy)

    def modal_forward(chunk):
        @pl.loop(edges[chunk], edges[chunk + 1])
        def _(tile):
            lanes = lanes_of(tile)
            log_row = jnp.log(decay_rows[pl.ds(tile, 1)])
            fill_modal_table(table, log_row, residue_rows[pl.ds(tile, 1)], modes, False)
            step = jnp.exp(log_rows[:, lanes] * NEAR)
            carried = entering[:, lanes]
            befores = []
            for b in range(blocks):
                wide[0:NEAR, LANES * b : LANES * (b + 1)] = product(
                    key_modal[block_rows(b), lanes], medium_out[block_rows(b), lanes]
                )
                befores.append(carried)
                carried = step * carried + end_states[b, :, lanes]
            parts = modal_blocks(table, wide, jnp.concatenate(befores, axis=1))
            for b in range(blocks):
                rows = block_rows(b)
                stage3[rows, lanes] = (cotangent[rows, lanes].astype(f32) * parts[b]).astype(bf16)

        send_home(3, stage3, out3, chunk)

    early_width = edges[2] * LANES
    first = Join(place, True, 0, early_width, own_total, entering, log_rows,
                 pair_f, y_f, x_f, o_f, (join_send, join_recv))
    second = Join(place, True, early_width, channels - early_width, own_total, entering, log_rows,
                  pair_s, y_s, x_s, o_s, (join2_send, join2_recv))
    backward = Join(place, False, 0, channels, own_adjoint, arriving, log_rows,
                    pair_b, y_b, x_b, o_b, (back_send, back_recv))
    medium_forward(0)
    medium_forward(1)
    first.start()
    medium_forward(2)
    first.along_y()
    medium_forward(3)
    first.along_x()
    medium_forward(4)
    second.start()
    first.share()
    cot_own.wait()
    loads[4].wait()
    adjoint_states(0)
    second.along_y()
    adjoint_states(1)
    first.end()
    modal_forward(0)
    second.along_x()
    modal_forward(1)
    second.share()
    adjoint_states(2)
    adjoint_states(3)
    adjoint_states(4)
    backward.start()
    second.end()
    modal_forward(2)
    backward.along_y()
    modal_forward(3)
    backward.along_x()
    modal_forward(4)
    backward.share()
    backward.end()

    head_copies = []
    for chunk in range(CHUNKS):

        @pl.loop(edges[chunk], edges[chunk + 1])
        def _(tile):
            lanes = lanes_of(tile)
            log_row = jnp.log(decay_rows[pl.ds(tile, 1)])
            fill_modal_table(table, log_row, residue_rows[pl.ds(tile, 1)], modes, True)
            step = jnp.exp(log_rows[:, lanes] * NEAR)
            carried = arriving[:, lanes]
            nexts = [carried] * blocks
            for b in reversed(range(blocks)):
                wide[0:NEAR, LANES * b : LANES * (b + 1)] = product(
                    cotangent[block_rows(b), lanes], query_modal[block_rows(b), lanes]
                )
                nexts[b] = carried
                carried = step * carried + start_states[b, :, lanes]
            parts = modal_blocks(table, wide, jnp.concatenate(nexts, axis=1))
            for b in range(blocks):
                rows = block_rows(b)
                stage4[rows, lanes] = (parts[b] * medium_out[rows, lanes].astype(f32)).astype(bf16)
                grad_out = parts[b] * key_modal[rows, lanes].astype(f32)
                stage0[rows, lanes] = (grad_out * conv[rows, lanes]).astype(bf16)
                grad_conv[rows, lanes] = (grad_out * query[rows, lanes].astype(f32)).astype(bf16)

        copy = remote(
            grad_conv.at[pl.ds(0, TAPS), columns(chunk)],
            grad_conv.at[pl.ds(row_count, TAPS), columns(chunk)],
            (head_send, head_recv), chunk, {"ctx": previous},
        )
        copy.start()
        head_copies.append(copy)
        send_home(4, stage4, out4, chunk)
        send_home(0, stage0, out0, chunk)

    flip = jnp.where(ramp(0) + ramp(1) == NEAR - 1, 1.0, 0.0)

    @pl.loop(0, tiles)
    def _(tile):
        lanes = lanes_of(tile)
        grads = jnp.concatenate([grad_conv[block_rows(b), lanes] for b in range(blocks)], axis=1)
        flipped = dot(flip.astype(bf16), grads)
        group = lane_group(NEAR, blocks * LANES)
        for g in range(TILE_GROUPS):
            left[block_rows(g)] = jnp.where(group == g, flipped, 0.0).astype(bf16)
        right = jnp.concatenate(
            [medium_input[NEAR * b : NEAR * (b + 2), lanes] for b in range(blocks)], axis=1
        )
        products = lax.dot_general(
            left[...], right, (((1,), (1,)), ((), ())), preferred_element_type=f32
        )
        rows = []
        for g in range(TILE_GROUPS):
            turned = pltpu.roll(products[block_rows(g)], 0, 1, stride=1, stride_axis=0)
            rows.append(jnp.sum(turned[:, NEAR:], axis=0, keepdims=True))
        sums[pl.ds(pl.multiple_of(tile * TILE_GROUPS, TILE_GROUPS), TILE_GROUPS)] = (
            jnp.concatenate(rows, axis=0)
        )

    core_sums[place.core] = sums[...]
    sum_sems = (sum_send, sum_recv)
    sum_copies = gather(core_sums, place.core, [place.partner], sum_sems, 0)

    for chunk in range(CHUNKS):
        head_copies[chunk].wait_recv()

        @pl.when(me == devices - 1)
        def _():
            grad_conv[row_count:, columns(chunk)] = jnp.zeros((TAPS, width(chunk)), bf16)

        @pl.loop(edges[chunk], edges[chunk + 1])
        def _(tile):
            lanes = lanes_of(tile)
            fill_medium_table(table, adjoint_row, tile)
            for pair in range(blocks // 2):
                both = medium_pair(table, grad_conv, lanes, pair)
                for half in range(2):
                    rows = block_rows(2 * pair + half)
                    grad_input = both[:, LANES * half : LANES * (half + 1)]
                    stage1[rows, lanes] = (grad_input * value[rows, lanes].astype(f32)).astype(bf16)
                    stage2[rows, lanes] = (grad_input * key[rows, lanes].astype(f32)).astype(bf16)

        send_home(1, stage1, out1, chunk)
        send_home(2, stage2, out2, chunk)
        if chunk == 0:
            finish(sum_copies)
            y_sums[place.y] = core_sums[0] + core_sums[1]
            sum_copies = gather(y_sums, place.y, place.y_peers, sum_sems, 1)
        if chunk == 1:
            finish(sum_copies)
            x_sums[place.x] = sum(y_sums[s] for s in range(1, place.size_y)) + y_sums[0]
            sum_copies = gather(x_sums, place.x, place.x_peers, sum_sems, place.size_y)
    finish(sum_copies)
    summed = sum(x_sums[s] for s in range(1, place.size_x)) + x_sums[0]
    filter_out[...] = (
        jnp.dot(summed, flip, precision=highest, preferred_element_type=f32) * scale
    )

    for copy in cot_copies + tail_copies + head_copies:
        copy.wait_send()
    for copy in own_copies:
        copy.wait()
    finish(out_copies)


def store_kernel(*refs):
    sems = refs[-1]
    count = (len(refs) - 1) // 2
    copies = [
        pltpu.make_async_copy(refs[n], refs[count + n], sems.at[n]) for n in range(count)
    ]
    for copy in copies:
        copy.start()
    for copy in copies:
        copy.wait()


def on_device(
    sizes, grad_out, query_medium, key_medium, value_medium, query_modal, key_modal,
    medium_filter, modal_decay, modal_residue,
):
    row_count, channels = query_medium.shape
    blocks = row_count // NEAR
    groups, modes = modal_decay.shape
    devices = lax.axis_size("ctx")
    size_z = lax.axis_size("ch")
    size_x, size_y, _ = sizes
    output = jax.ShapeDtypeStruct(grad_out.shape, bf16)
    filter_output = jax.ShapeDtypeStruct((groups, TAPS), f32)
    scale = 1.0 / math.sqrt(row_count * devices * GS)
    data = pltpu.VMEM((row_count, channels), bf16)
    longer = pltpu.VMEM((row_count + TAPS, channels), bf16)
    states = pltpu.VMEM((blocks, modes, channels), f32)
    state = pltpu.VMEM((modes, channels), f32)

    early_width = channels * BOUNDS[2] // BOUNDS[-1]

    def joins(width):
        return [pltpu.VMEM((n, modes, width // 2), f32) for n in (2, size_y, size_x, 2)]

    dma = pltpu.SemaphoreType.DMA
    square = (groups, TAPS)
    whole = pl.BlockSpec(memory_space=pl.ANY)
    local = pl.BlockSpec(memory_space=pltpu.VMEM)
    outs = pl.pallas_call(
        lambda *refs: whole_kernel(sizes, scale, *refs),
        in_specs=[whole] * 6 + [local] * 3,
        out_shape=(pltpu.VMEM(grad_out.shape, bf16),) * 5 + (pltpu.VMEM((groups, TAPS), f32),),
        out_specs=(local,) * 6,
        scratch_shapes=[data] * 6
        + [longer, pltpu.VMEM((row_count, channels), f32), data, longer]
        + [data] * 5
        + [states] * 2 + [state] * 5
        + joins(early_width) + joins(channels - early_width) + joins(channels)
        + [pltpu.VMEM((groups * modes // LANES, LANES), f32)] * 2
        + [pltpu.VMEM((groups, 2 * TAPS), f32)] * 2
        + [pltpu.VMEM((TILE_GROUPS * NEAR, 2 * NEAR), bf16),
           pltpu.VMEM((2 * NEAR, blocks * LANES), bf16),
           pltpu.VMEM((TILE_GROUPS * NEAR, blocks * LANES), bf16)]
        + [pltpu.VMEM(square, f32)]
        + [pltpu.VMEM((n,) + square, f32) for n in (2, size_y, size_x)]
        + [dma((5,))] + [dma((size_z - 1, CHUNKS))] * 2 + [dma((CHUNKS,))] * 4
        + [dma((size_x + size_y,))] * 6 + [dma((size_x + size_y,))] * 2
        + [dma((5, size_z - 1, CHUNKS))] * 2 + [dma((6,))],
        compiler_params=pltpu.CompilerParams(
            collective_id=0, has_side_effects=True, vmem_limit_bytes=48 * 1024 * 1024
        ),
    )(
        grad_out, query_medium, key_medium, value_medium, query_modal, key_modal,
        medium_filter, modal_decay.T, modal_residue.T,
    )
    stored = pl.pallas_call(
        store_kernel,
        in_specs=[local] * 6,
        out_shape=(output,) * 5 + (filter_output,),
        out_specs=(whole,) * 6,
        scratch_shapes=[dma((6,))],
        compiler_params=pltpu.CompilerParams(vmem_limit_bytes=2 * 1024 * 1024),
    )(*[pltpu.with_memory_space_constraint(out, pltpu.VMEM) for out in outs])
    return tuple(stored)


def solution(mesh):
    count = mesh.shape["ctx"] // 2
    side = math.isqrt(count)
    sizes = (side, count // side, 2)

    def body(*args):
        return on_device(sizes, *args)

    rows = P(("ctx", "ch"), None)
    groups = P("ch", None)
    return jax.shard_map(
        body,
        mesh=mesh,
        in_specs=(rows,) + (P("ctx", "ch"),) * 5 + (groups,) * 3,
        out_specs=(rows,) * 5 + (groups,),
        check_vma=False,
    )
```
